256 devices in a mesh: grp: 4 (over x_lo, core), row: 4 (over y), col: 16 (over z, x_hi).
Axes of the slice: x: 4 (x_hi: 2, x_lo: 2; x = x_hi * 2 + x_lo), y: 4, z: 8, core: 2. Of those that a mesh axis runs over, the one named last changes fastest.
Arguments:
- block_rows: bfloat16 [8, 304, 10240], P('grp', None, ('row', 'col')), may hold values from -6 to 6
- inverse_factor: float32 [8, 304, 304], P('grp'), as said below
- live_rows: int32 [8], P('grp'), may hold values from 50 to 304, as said below
- shift: float32 [10240], P(('grp', 'row', 'col')), may hold values from 0.5 to 2
Outputs:
- factored: float32 [10240, 10240], P(('grp', 'row'), 'col')
The draws below stay inside these ranges and needn't reach their ends.
Inputs may be any that keep to these rules, and one draw needn't show every extreme that they name: `live_rows`: every block uses between 50 and 304 rows; some block uses exactly 304 and some exactly 50. `inverse_factor`: each block's matrix is lower triangular with a positive diagonal.
All inputs are finite; a program needn't handle non-finite values.
Results may differ from the reference program's by a relative error of at most 0.0043.
Values may be sent and summed in bfloat16 or wider, within the bound.
A program may use at most 128 MiB of HBM per device.

```python
import math
import jax
import jax.numpy as jnp
from jax import lax

N = 10240
PW = 1024
PMAX = 304
PANELS = 1
BLOCKS = 8
NPAN = 10
SLAB = 64
TWIN = 4
N_GRP = 4
N_ROW = 4
N_COL = 16


def draw_inverse_factor(key, part):
    first_key, second_key = jax.random.split(jax.random.fold_in(key, 11))
    overall = 2.0 / math.sqrt(BLOCKS * PMAX)
    diagonal = jax.random.uniform(first_key, (BLOCKS, PMAX), jnp.float32, 0.5, 1.5)
    below = jax.random.normal(second_key, (BLOCKS, PMAX, PMAX), jnp.float32) * (0.4 / math.sqrt(PMAX))
    identity = jnp.eye(PMAX, dtype=jnp.float32)
    triangle = jnp.tril(below, -1) + diagonal[:, :, None] * identity[None, :, :]
    return (triangle * overall).astype(jnp.float32)


def draw_live_rows(key, part):
    first_key, second_key = jax.random.split(jax.random.fold_in(key, 23))
    counts = jax.random.randint(first_key, (BLOCKS,), PMAX // 6, PMAX + 1)
    spot = jax.random.randint(second_key, (), 0, BLOCKS)
    ordinal = jnp.arange(BLOCKS, dtype=jnp.int32)
    counts = jnp.where(ordinal == spot, PMAX, counts)
    counts = jnp.where(ordinal == (spot + 1) % BLOCKS, PMAX // 6, counts)
    return counts.astype(jnp.int32)


def block_levels(stream_key, shape, pieces, smallest, high):
    def one(dim, parts):
        heights = jax.random.uniform(jax.random.fold_in(jax.random.fold_in(stream_key, 6), dim), (parts,), jnp.float32, smallest / len(pieces), high / len(pieces))
        return jnp.repeat(jnp.exp(heights), shape[dim] // parts).reshape((-1,) + (1,) * (len(shape) - dim - 1))

    level = one(*pieces[0])
    for cut in pieces[1:]:
        level = level * one(*cut)
    return level


def scatter_about(stream_key, extent, width, limit, cuts=(), held_as=jnp.bfloat16):
    values = jax.random.normal(stream_key, extent, jnp.float32) * width
    if len(cuts) > 0:
        values = block_levels(stream_key, extent, cuts, -0.22, 0.18) * values
    return jnp.clip(values, min=-limit, max=limit).astype(held_as)


def setup_inputs(seed: int = 0) -> dict:
    splits = jax.random.split(jax.random.key(seed), 5)
    return {
        "block_rows": scatter_about(splits[0], (BLOCKS, PMAX, N), 1.0, 6.0, ((0, 4), (2, 64))),
        "inverse_factor": draw_inverse_factor(jax.random.fold_in(splits[4], 71), 0),
        "live_rows": draw_live_rows(jax.random.fold_in(splits[4], 71), 0),
        "shift": jnp.clip(0.5 + 1.5 * jax.random.uniform(splits[3], (N,), jnp.float32) ** block_levels(splits[3], (N,), ((0, 256),), -0.2, 0.2), 0.5, 2.0),
    }


def reference(block_rows, inverse_factor, live_rows, shift):
    highest = lax.Precision.HIGHEST
    ordinal = jnp.arange(PMAX, dtype=jnp.int32)
    live_mask = (ordinal[None, :] < live_rows[:, None]).astype(jnp.float32)
    masked_factor = inverse_factor * live_mask[:, :, None] * live_mask[:, None, :]
    natural_rows = block_rows.astype(jnp.float32).reshape(BLOCKS, PMAX, N_ROW, N_COL, N_GRP, NPAN, TWIN)
    natural_rows = jnp.transpose(natural_rows, (0, 1, 5, 4, 2, 3, 6)).reshape(BLOCKS, PMAX, N)
    whitened = jnp.einsum('bij,bjm->bim', masked_factor, natural_rows, precision=highest)
    whitened = whitened.astype(jnp.bfloat16).reshape(BLOCKS * PMAX, N)
    schur_sum = lax.dot_general(whitened.astype(jnp.float32), whitened.astype(jnp.float32), (((0,), (0,)), ((), ())), preferred_element_type=jnp.float32)
    shift_nat = jnp.transpose(shift.reshape(N_GRP, N_ROW, N_COL, NPAN, TWIN), (3, 0, 1, 2, 4)).reshape(N)
    matrix = schur_sum + jnp.diag(shift_nat)
    index = jnp.arange(N, dtype=jnp.int32)
    finished = []
    for panel in range(PANELS):
        first = panel * PW
        beyond = (panel + 1) * PW
        cholesky_factor = jnp.linalg.cholesky(matrix[first:beyond, first:beyond])
        solved = jax.scipy.linalg.solve_triangular(cholesky_factor, matrix[:, first:beyond].T, lower=True).T
        finished.append(jnp.where(index[:, None] >= index[None, first:beyond], solved, 0.0))
        trailing_part = solved[beyond:]
        update = jnp.dot(trailing_part.astype(jnp.float32), trailing_part.T.astype(jnp.float32), precision=highest, preferred_element_type=jnp.float32)
        matrix = matrix.at[beyond:, beyond:].add(-update)
    boundary = PANELS * PW
    trailing = jnp.where(index[:, None] >= boundary, matrix[:, boundary:], 0.0)
    whole = jnp.concatenate(finished + [trailing], axis=1)
    whole = whole.reshape(NPAN, N_GRP, N_ROW, SLAB, NPAN, N_GRP, N_ROW, N_COL, TWIN)
    whole = jnp.transpose(whole, (1, 2, 0, 3, 7, 4, 5, 6, 8))
    return whole.reshape(N, N)
```

```python
import jax
import jax.numpy as jnp
from jax import lax
from jax.sharding import PartitionSpec as P

PW = 1024
PANELS = 1
NPAN = 10


def local(block_rows, inverse_factor, live_rows, shift):
    highest = lax.Precision.HIGHEST
    groups = lax.axis_size("grp")
    rowcount = lax.axis_size("row")
    colcount = lax.axis_size("col")
    owners = groups * rowcount
    slab = PW // owners
    window = slab // colcount
    group_index = lax.axis_index("grp")
    row_index = lax.axis_index("row")
    col_index = lax.axis_index("col")
    blocks, padded, local_cols = block_rows.shape
    stacked = blocks * padded
    total = stacked * groups
    n_all = NPAN * owners * slab

    ordinal = jnp.arange(padded, dtype=jnp.int32)
    live_mask = (ordinal[None, :] < live_rows[:, None]).astype(jnp.float32)
    masked_factor = inverse_factor * live_mask[:, :, None] * live_mask[:, None, :]
    whitened = jnp.einsum(
        "bij,bjm->mbi", masked_factor, block_rows.astype(jnp.float32), precision=highest
    )
    whitened = whitened.astype(jnp.bfloat16).reshape(local_cols, stacked)

    every = lax.all_gather(whitened, "grp", axis=0, tiled=False)
    every = jnp.transpose(every, (1, 0, 2)).reshape(groups, NPAN, window, total)

    panel_w = every[:, 0]
    panel_w = lax.all_gather(panel_w, "col", axis=0, tiled=False)
    panel_w = lax.all_gather(panel_w, "row", axis=0, tiled=False)
    every, panel_w = lax.optimization_barrier((every, panel_w))
    panel_w = jnp.transpose(panel_w, (2, 0, 1, 3, 4)).reshape(PW, total)

    row_w = lax.dynamic_index_in_dim(every, group_index, 0, keepdims=False)
    row_w = lax.all_gather(row_w, "col", axis=0, tiled=False)
    row_w = jnp.transpose(row_w, (1, 0, 2, 3)).reshape(NPAN * colcount * window, total)

    col_w = lax.all_gather(every, "row", axis=0, tiled=False)
    col_w = jnp.transpose(col_w, (2, 1, 0, 3, 4)).reshape(NPAN * owners * window, total)

    shift_all = lax.all_gather(shift, ("grp", "row", "col"), axis=0, tiled=True)
    shift_nat = jnp.transpose(
        shift_all.reshape(groups, rowcount, colcount, NPAN, window), (3, 0, 1, 2, 4)
    ).reshape(n_all)

    panel_ids = jnp.arange(NPAN, dtype=jnp.int32)
    slab_ids = jnp.arange(slab, dtype=jnp.int32)
    owner_ids = jnp.arange(owners, dtype=jnp.int32)
    window_ids = jnp.arange(window, dtype=jnp.int32)
    own_owner = group_index * rowcount + row_index
    row_global = ((panel_ids[:, None] * owners + own_owner) * slab + slab_ids[None, :]).reshape(-1)
    col_global = (
        (panel_ids[:, None, None] * owners + owner_ids[None, :, None]) * slab
        + col_index * window
        + window_ids[None, None, :]
    ).reshape(-1)
    panel_ids_all = jnp.arange(PW, dtype=jnp.int32)
    shift_panel = shift_nat[:PW]

    dims = (((1,), (1,)), ((), ()))
    f32 = jnp.float32
    diag_block = lax.dot_general(panel_w, panel_w, dims, preferred_element_type=f32)
    diag_block = diag_block + jnp.where(
        panel_ids_all[:, None] == panel_ids_all[None, :], shift_panel[None, :], 0.0
    )
    both_w = jnp.concatenate([row_w, col_w], axis=0)
    both_global = jnp.concatenate([row_global, col_global], axis=0)
    both_panel = lax.dot_general(both_w, panel_w, dims, preferred_element_type=f32)
    both_panel = both_panel + jnp.where(
        both_global[:, None] == panel_ids_all[None, :], shift_panel[None, :], 0.0
    )
    schur_tile = lax.dot_general(row_w, col_w, dims, preferred_element_type=f32)
    schur_tile = schur_tile + jnp.where(
        row_global[:, None] == col_global[None, :], shift_nat[col_global][None, :], 0.0
    )

    cholesky_factor = jnp.linalg.cholesky(diag_block)
    solved = lax.linalg.triangular_solve(
        cholesky_factor, both_panel, left_side=False, lower=True, transpose_a=True
    )
    local_rows = row_global.shape[0]
    row_factor = solved[:local_rows]
    col_factor = solved[local_rows:]

    panel_piece = lax.dynamic_slice_in_dim(
        row_factor.reshape(local_rows, owners, slab), col_index * window, window, 2
    ).reshape(local_rows, owners * window)
    panel_cols_global = col_global.reshape(NPAN, -1)[0]
    finished = jnp.where(row_global[:, None] >= panel_cols_global[None, :], panel_piece, 0.0)

    boundary = PANELS * PW
    first_trailing = owners * window
    update = jnp.dot(
        row_factor, col_factor[first_trailing:].T, precision=highest, preferred_element_type=f32
    )
    trailing = schur_tile[:, first_trailing:] - update
    trailing = jnp.where(row_global[:, None] >= boundary, trailing, 0.0)
    return jnp.concatenate([finished, trailing], axis=1)


def solution(mesh):
    in_specs = (
        P("grp", None, ("row", "col")),
        P("grp", None, None),
        P("grp"),
        P(("grp", "row", "col")),
    )
    out_specs = P(("grp", "row"), "col")
    return jax.shard_map(local, mesh=mesh, in_specs=in_specs, out_specs=out_specs, check_vma=False)
```

```python
import jax
import jax.numpy as jnp
from jax import lax
from jax.sharding import PartitionSpec as P

PW = 1024
PANELS = 1
NPAN = 10


def split3(x):
    hi = lax.reduce_precision(x, exponent_bits=8, mantissa_bits=7)
    rest = x - hi
    mid = lax.reduce_precision(rest, exponent_bits=8, mantissa_bits=7)
    lo = rest - mid
    return jnp.concatenate([hi, mid, lo]).astype(jnp.bfloat16)


def join3(parts):
    parts = parts.astype(jnp.float32).reshape(parts.shape[:-1] + (3, -1))
    return (parts[..., 0, :] + parts[..., 1, :]) + parts[..., 2, :]


def local(block_rows, inverse_factor, live_rows, shift):
    highest = lax.Precision.HIGHEST
    groups = lax.axis_size("grp")
    rowcount = lax.axis_size("row")
    colcount = lax.axis_size("col")
    owners = groups * rowcount
    slab = PW // owners
    window = slab // colcount
    group_index = lax.axis_index("grp")
    row_index = lax.axis_index("row")
    col_index = lax.axis_index("col")
    blocks, padded, local_cols = block_rows.shape
    stacked = blocks * padded
    total = stacked * groups

    ordinal = jnp.arange(padded, dtype=jnp.int32)
    live_mask = (ordinal[None, :] < live_rows[:, None]).astype(jnp.float32)
    masked_factor = inverse_factor * live_mask[:, :, None] * live_mask[:, None, :]
    whitened = jnp.einsum(
        "bij,bjm->mbi", masked_factor, block_rows.astype(jnp.float32), precision=highest
    )
    whitened = whitened.astype(jnp.bfloat16).reshape(local_cols, stacked)

    shift_row = jnp.zeros((1, stacked), jnp.bfloat16).at[0, : 3 * shift.shape[0]].set(
        split3(shift)
    )
    every = lax.all_gather(
        jnp.concatenate([whitened, shift_row], axis=0), "grp", axis=0, tiled=False
    )
    shift_grp = join3(every[:, local_cols, : 3 * shift.shape[0]]).reshape(groups, NPAN, window)
    every = jnp.transpose(every[:, :local_cols], (1, 0, 2)).reshape(groups, NPAN, window, total)

    panel_shift_row = jnp.zeros((1, total), jnp.bfloat16).at[0, : 3 * groups * window].set(
        split3(shift_grp[:, 0].reshape(-1))
    )
    panel_w = jnp.concatenate([every[:, 0].reshape(groups * window, total), panel_shift_row], 0)
    panel_w = lax.all_gather(panel_w, "col", axis=0, tiled=False)
    panel_w = lax.all_gather(panel_w, "row", axis=0, tiled=False)
    every, panel_w = lax.optimization_barrier((every, panel_w))
    shift_panel = join3(panel_w[:, :, groups * window, : 3 * groups * window])
    shift_panel = jnp.transpose(
        shift_panel.reshape(rowcount, colcount, groups, window), (2, 0, 1, 3)
    ).reshape(PW)
    panel_w = panel_w[:, :, : groups * window].reshape(rowcount, colcount, groups, window, total)
    panel_w = jnp.transpose(panel_w, (2, 0, 1, 3, 4)).reshape(PW, total)

    row_w = lax.dynamic_index_in_dim(every, group_index, 0, keepdims=False)
    row_w = lax.all_gather(row_w, "col", axis=0, tiled=False)
    row_w = jnp.transpose(row_w, (1, 0, 2, 3)).reshape(NPAN * colcount * window, total)

    col_w = lax.all_gather(every, "row", axis=0, tiled=False)
    col_w = jnp.transpose(col_w, (2, 1, 0, 3, 4)).reshape(NPAN * owners * window, total)

    panel_ids = jnp.arange(NPAN, dtype=jnp.int32)
    slab_ids = jnp.arange(slab, dtype=jnp.int32)
    owner_ids = jnp.arange(owners, dtype=jnp.int32)
    window_ids = jnp.arange(window, dtype=jnp.int32)
    own_owner = group_index * rowcount + row_index
    row_global = ((panel_ids[:, None] * owners + own_owner) * slab + slab_ids[None, :]).reshape(-1)
    col_global = (
        (panel_ids[:, None, None] * owners + owner_ids[None, :, None]) * slab
        + col_index * window
        + window_ids[None, None, :]
    ).reshape(-1)
    panel_ids_all = jnp.arange(PW, dtype=jnp.int32)
    shift_col = jnp.broadcast_to(
        shift.reshape(NPAN, 1, window), (NPAN, owners, window)
    ).reshape(-1)

    dims = (((1,), (1,)), ((), ()))
    f32 = jnp.float32
    diag_block = lax.dot_general(panel_w, panel_w, dims, preferred_element_type=f32)
    diag_block = diag_block + jnp.where(
        panel_ids_all[:, None] == panel_ids_all[None, :], shift_panel[None, :], 0.0
    )
    both_w = jnp.concatenate([row_w, col_w], axis=0)
    both_global = jnp.concatenate([row_global, col_global], axis=0)
    both_panel = lax.dot_general(both_w, panel_w, dims, preferred_element_type=f32)
    both_panel = both_panel + jnp.where(
        both_global[:, None] == panel_ids_all[None, :], shift_panel[None, :], 0.0
    )
    schur_tile = lax.dot_general(row_w, col_w, dims, preferred_element_type=f32)
    schur_tile = schur_tile + jnp.where(
        row_global[:, None] == col_global[None, :], shift_col[None, :], 0.0
    )

    cholesky_factor = jnp.linalg.cholesky(diag_block)
    solved = lax.linalg.triangular_solve(
        cholesky_factor, both_panel, left_side=False, lower=True, transpose_a=True
    )
    local_rows = row_global.shape[0]
    row_factor = solved[:local_rows]
    col_factor = solved[local_rows:]

    panel_piece = lax.dynamic_slice_in_dim(
        row_factor.reshape(local_rows, owners, slab), col_index * window, window, 2
    ).reshape(local_rows, owners * window)
    panel_cols_global = col_global.reshape(NPAN, -1)[0]
    finished = jnp.where(row_global[:, None] >= panel_cols_global[None, :], panel_piece, 0.0)

    boundary = PANELS * PW
    first_trailing = owners * window
    update = jnp.dot(
        row_factor, col_factor[first_trailing:].T, precision=highest, preferred_element_type=f32
    )
    trailing = schur_tile[:, first_trailing:] - update
    trailing = jnp.where(row_global[:, None] >= boundary, trailing, 0.0)
    return jnp.concatenate([finished, trailing], axis=1)


def solution(mesh):
    in_specs = (
        P("grp", None, ("row", "col")),
        P("grp", None, None),
        P("grp"),
        P(("grp", "row", "col")),
    )
    out_specs = P(("grp", "row"), "col")
    return jax.shard_map(local, mesh=mesh, in_specs=in_specs, out_specs=out_specs, check_vma=False)
```

```python
import functools

import jax
import jax.numpy as jnp
from jax import lax
from jax.experimental import pallas as pl
from jax.experimental.pallas import tpu as pltpu
from jax.sharding import PartitionSpec as P

PW = 1024
PANELS = 1
NPAN = 10
HI = lax.Precision.HIGHEST


def _base_inverse(s):
    b = s.shape[0]
    lane = lax.broadcasted_iota(jnp.int32, (b, b), 1)
    sub = lax.broadcasted_iota(jnp.int32, (b, b), 0)
    sub_col = lax.broadcasted_iota(jnp.int32, (b, 1), 0)
    lane_row = lax.broadcasted_iota(jnp.int32, (1, b), 1)
    eye = jnp.where(lane == sub, 1.0, 0.0).astype(jnp.float32)

    def step(j, carry):
        work, inv = carry
        col = jnp.sum(jnp.where(lane == j, work, 0.0), axis=1, keepdims=True)
        row = jnp.sum(jnp.where(sub == j, work, 0.0), axis=0, keepdims=True)
        pivot = jnp.sum(jnp.where(lane_row == j, row, 0.0), axis=1, keepdims=True)
        scale = lax.rsqrt(pivot)
        l_col = jnp.where(sub_col >= j, col * scale, 0.0)
        l_row = jnp.where(lane_row >= j, row * scale, 0.0)
        work = work - l_col * l_row
        inv_row = jnp.sum(jnp.where(sub == j, inv, 0.0), axis=0, keepdims=True)
        diag = pivot * scale
        u = jnp.where(sub_col == j, l_col - 1.0, l_col) / diag
        inv = inv - u * inv_row
        return work, inv

    _, inv = lax.fori_loop(0, b, step, (s, eye))
    return inv


def _kernel(a_ref, z_ref, *, n, b):
    z_ref[...] = jnp.zeros_like(z_ref)
    for k in range(n // b):
        lo = k * b
        s = a_ref[lo:lo + b, lo:lo + b]
        if k > 0:
            zk = z_ref[0:lo, 0:lo]
            left = lax.dot_general(a_ref[lo:lo + b, 0:lo], zk, (((1,), (1,)), ((), ())),
                                   precision=HI, preferred_element_type=jnp.float32)
            s = s - lax.dot_general(left, left, (((1,), (1,)), ((), ())),
                                    precision=HI, preferred_element_type=jnp.float32)
        d = _base_inverse(s)
        z_ref[lo:lo + b, lo:lo + b] = d
        if k > 0:
            t = jnp.dot(left, zk, precision=HI, preferred_element_type=jnp.float32)
            z_ref[lo:lo + b, 0:lo] = -jnp.dot(d, t, precision=HI, preferred_element_type=jnp.float32)


def inverse_cholesky(a, b=128):
    n = a.shape[0]
    return pl.pallas_call(
        functools.partial(_kernel, n=n, b=b),
        out_shape=jax.ShapeDtypeStruct((n, n), jnp.float32),
        in_specs=[pl.BlockSpec(memory_space=pltpu.VMEM)],
        out_specs=pl.BlockSpec(memory_space=pltpu.VMEM),
        compiler_params=pltpu.CompilerParams(vmem_limit_bytes=48 * 1024 * 1024),
        cost_estimate=pl.CostEstimate(
            flops=2 * n * n * n, transcendentals=n, bytes_accessed=8 * n * n
        ),
    )(a)


def split3(x):
    hi = lax.reduce_precision(x, exponent_bits=8, mantissa_bits=7)
    rest = x - hi
    mid = lax.reduce_precision(rest, exponent_bits=8, mantissa_bits=7)
    lo = rest - mid
    return jnp.concatenate([hi, mid, lo]).astype(jnp.bfloat16)


def join3(parts):
    parts = parts.astype(jnp.float32).reshape(parts.shape[:-1] + (3, -1))
    return (parts[..., 0, :] + parts[..., 1, :]) + parts[..., 2, :]


def local(block_rows, inverse_factor, live_rows, shift):
    highest = lax.Precision.HIGHEST
    groups = lax.axis_size("grp")
    rowcount = lax.axis_size("row")
    colcount = lax.axis_size("col")
    owners = groups * rowcount
    slab = PW // owners
    window = slab // colcount
    group_index = lax.axis_index("grp")
    row_index = lax.axis_index("row")
    col_index = lax.axis_index("col")
    blocks, padded, local_cols = block_rows.shape
    stacked = blocks * padded
    total = stacked * groups

    ordinal = jnp.arange(padded, dtype=jnp.int32)
    live_mask = (ordinal[None, :] < live_rows[:, None]).astype(jnp.float32)
    masked_factor = inverse_factor * live_mask[:, :, None] * live_mask[:, None, :]
    whitened = jnp.einsum(
        "bij,bjm->mbi", masked_factor, block_rows.astype(jnp.float32), precision=highest
    )
    whitened = whitened.astype(jnp.bfloat16).reshape(local_cols, stacked)

    shift_row = jnp.zeros((1, stacked), jnp.bfloat16).at[0, : 3 * shift.shape[0]].set(
        split3(shift)
    )
    every = lax.all_gather(
        jnp.concatenate([whitened, shift_row], axis=0), "grp", axis=0, tiled=False
    )
    shift_grp = join3(every[:, local_cols, : 3 * shift.shape[0]]).reshape(groups, NPAN, window)
    every = jnp.transpose(every[:, :local_cols], (1, 0, 2)).reshape(groups, NPAN, window, total)

    panel_shift_row = jnp.zeros((1, total), jnp.bfloat16).at[0, : 3 * groups * window].set(
        split3(shift_grp[:, 0].reshape(-1))
    )
    panel_w = jnp.concatenate([every[:, 0].reshape(groups * window, total), panel_shift_row], 0)
    panel_w = lax.all_gather(panel_w, "col", axis=0, tiled=False)
    panel_w = lax.all_gather(panel_w, "row", axis=0, tiled=False)
    every, panel_w = lax.optimization_barrier((every, panel_w))
    shift_panel = join3(panel_w[:, :, groups * window, : 3 * groups * window])
    shift_panel = jnp.transpose(
        shift_panel.reshape(rowcount, colcount, groups, window), (2, 0, 1, 3)
    ).reshape(PW)
    panel_w = panel_w[:, :, : groups * window].reshape(rowcount, colcount, groups, window, total)
    panel_w = jnp.transpose(panel_w, (2, 0, 1, 3, 4)).reshape(PW, total)

    row_w = lax.dynamic_index_in_dim(every, group_index, 0, keepdims=False)
    row_w = lax.all_gather(row_w, "col", axis=0, tiled=False)
    row_w = jnp.transpose(row_w, (1, 0, 2, 3)).reshape(NPAN * colcount * window, total)

    col_w = lax.all_gather(every, "row", axis=0, tiled=False)
    col_w = jnp.transpose(col_w, (2, 1, 0, 3, 4)).reshape(NPAN * owners * window, total)

    panel_ids = jnp.arange(NPAN, dtype=jnp.int32)
    slab_ids = jnp.arange(slab, dtype=jnp.int32)
    owner_ids = jnp.arange(owners, dtype=jnp.int32)
    window_ids = jnp.arange(window, dtype=jnp.int32)
    own_owner = group_index * rowcount + row_index
    row_global = ((panel_ids[:, None] * owners + own_owner) * slab + slab_ids[None, :]).reshape(-1)
    col_global = (
        (panel_ids[:, None, None] * owners + owner_ids[None, :, None]) * slab
        + col_index * window
        + window_ids[None, None, :]
    ).reshape(-1)
    panel_ids_all = jnp.arange(PW, dtype=jnp.int32)
    shift_col = jnp.broadcast_to(
        shift.reshape(NPAN, 1, window), (NPAN, owners, window)
    ).reshape(-1)

    dims = (((1,), (1,)), ((), ()))
    f32 = jnp.float32
    diag_block = lax.dot_general(panel_w, panel_w, dims, preferred_element_type=f32)
    diag_block = diag_block + jnp.where(
        panel_ids_all[:, None] == panel_ids_all[None, :], shift_panel[None, :], 0.0
    )
    both_w = jnp.concatenate([row_w, col_w], axis=0)
    both_global = jnp.concatenate([row_global, col_global], axis=0)
    both_panel = lax.dot_general(both_w, panel_w, dims, preferred_element_type=f32)
    both_panel = both_panel + jnp.where(
        both_global[:, None] == panel_ids_all[None, :], shift_panel[None, :], 0.0
    )
    schur_tile = lax.dot_general(row_w, col_w, dims, preferred_element_type=f32)
    schur_tile = schur_tile + jnp.where(
        row_global[:, None] == col_global[None, :], shift_col[None, :], 0.0
    )

    inverse_factor_panel = inverse_cholesky(diag_block)
    solved = lax.dot_general(
        both_panel, inverse_factor_panel, dims, precision=highest, preferred_element_type=f32
    )
    local_rows = row_global.shape[0]
    row_factor = solved[:local_rows]
    col_factor = solved[local_rows:]

    panel_piece = lax.dynamic_slice_in_dim(
        row_factor.reshape(local_rows, owners, slab), col_index * window, window, 2
    ).reshape(local_rows, owners * window)
    panel_cols_global = col_global.reshape(NPAN, -1)[0]
    finished = jnp.where(row_global[:, None] >= panel_cols_global[None, :], panel_piece, 0.0)

    boundary = PANELS * PW
    first_trailing = owners * window
    update = jnp.dot(
        row_factor, col_factor[first_trailing:].T, precision=highest, preferred_element_type=f32
    )
    trailing = schur_tile[:, first_trailing:] - update
    trailing = jnp.where(row_global[:, None] >= boundary, trailing, 0.0)
    return jnp.concatenate([finished, trailing], axis=1)


def solution(mesh):
    in_specs = (
        P("grp", None, ("row", "col")),
        P("grp", None, None),
        P("grp"),
        P(("grp", "row", "col")),
    )
    out_specs = P(("grp", "row"), "col")
    return jax.shard_map(local, mesh=mesh, in_specs=in_specs, out_specs=out_specs, check_vma=False)
```

```python
import functools

import jax
import jax.numpy as jnp
from jax import lax
from jax.experimental import pallas as pl
from jax.experimental.pallas import tpu as pltpu
from jax.sharding import PartitionSpec as P

PW = 1024
PANELS = 1
NPAN = 10
HI = lax.Precision.HIGHEST


def _base_inverse(s):
    b = s.shape[0]
    lane = lax.broadcasted_iota(jnp.int32, (b, b), 1)
    sub = lax.broadcasted_iota(jnp.int32, (b, b), 0)
    sub_col = lax.broadcasted_iota(jnp.int32, (b, 1), 0)
    lane_row = lax.broadcasted_iota(jnp.int32, (1, b), 1)
    eye = jnp.where(lane == sub, 1.0, 0.0).astype(jnp.float32)

    def step(j, carry):
        work, inv = carry
        col = jnp.sum(jnp.where(lane == j, work, 0.0), axis=1, keepdims=True)
        row = jnp.sum(jnp.where(sub == j, work, 0.0), axis=0, keepdims=True)
        pivot = jnp.sum(jnp.where(lane_row == j, row, 0.0), axis=1, keepdims=True)
        scale = lax.rsqrt(pivot)
        l_col = jnp.where(sub_col >= j, col * scale, 0.0)
        l_row = jnp.where(lane_row >= j, row * scale, 0.0)
        work = work - l_col * l_row
        inv_row = jnp.sum(jnp.where(sub == j, inv, 0.0), axis=0, keepdims=True)
        diag = pivot * scale
        u = jnp.where(sub_col == j, l_col - 1.0, l_col) / diag
        inv = inv - u * inv_row
        return work, inv

    _, inv = lax.fori_loop(0, b, step, (s, eye))
    return inv


def _kernel(a_ref, z_ref, *, n, b):
    z_ref[...] = jnp.zeros_like(z_ref)
    for k in range(n // b):
        lo = k * b
        s = a_ref[lo:lo + b, lo:lo + b]
        if k > 0:
            zk = z_ref[0:lo, 0:lo]
            left = lax.dot_general(a_ref[lo:lo + b, 0:lo], zk, (((1,), (1,)), ((), ())),
                                   precision=HI, preferred_element_type=jnp.float32)
            s = s - lax.dot_general(left, left, (((1,), (1,)), ((), ())),
                                    precision=HI, preferred_element_type=jnp.float32)
        d = _base_inverse(s)
        z_ref[lo:lo + b, lo:lo + b] = d
        if k > 0:
            t = jnp.dot(left, zk, precision=HI, preferred_element_type=jnp.float32)
            z_ref[lo:lo + b, 0:lo] = -jnp.dot(d, t, precision=HI, preferred_element_type=jnp.float32)


def inverse_cholesky(a, b=128):
    n = a.shape[0]
    return pl.pallas_call(
        functools.partial(_kernel, n=n, b=b),
        out_shape=jax.ShapeDtypeStruct((n, n), jnp.float32),
        in_specs=[pl.BlockSpec(memory_space=pltpu.VMEM)],
        out_specs=pl.BlockSpec(memory_space=pltpu.VMEM),
        compiler_params=pltpu.CompilerParams(vmem_limit_bytes=48 * 1024 * 1024),
        cost_estimate=pl.CostEstimate(
            flops=2 * n * n * n, transcendentals=n, bytes_accessed=8 * n * n
        ),
    )(a)


def split3(x):
    hi = lax.reduce_precision(x, exponent_bits=8, mantissa_bits=7)
    rest = x - hi
    mid = lax.reduce_precision(rest, exponent_bits=8, mantissa_bits=7)
    lo = rest - mid
    return jnp.concatenate([hi, mid, lo]).astype(jnp.bfloat16)


def join3(parts):
    parts = parts.astype(jnp.float32).reshape(parts.shape[:-1] + (3, -1))
    return (parts[..., 0, :] + parts[..., 1, :]) + parts[..., 2, :]


def local(block_rows, inverse_factor, live_rows, shift):
    highest = lax.Precision.HIGHEST
    groups = lax.axis_size("grp")
    rowcount = lax.axis_size("row")
    colcount = lax.axis_size("col")
    owners = groups * rowcount
    slab = PW // owners
    window = slab // colcount
    group_index = lax.axis_index("grp")
    row_index = lax.axis_index("row")
    col_index = lax.axis_index("col")
    blocks, padded, local_cols = block_rows.shape
    stacked = blocks * padded
    total = stacked * groups

    ordinal = jnp.arange(padded, dtype=jnp.int32)
    live_mask = (ordinal[None, :] < live_rows[:, None]).astype(jnp.float32)
    masked_factor = inverse_factor * live_mask[:, :, None] * live_mask[:, None, :]
    whitened = jnp.einsum(
        "bij,bjm->mbi", masked_factor, block_rows.astype(jnp.float32), precision=highest
    )
    whitened = whitened.astype(jnp.bfloat16).reshape(local_cols, stacked)

    shift_row = jnp.zeros((1, stacked), jnp.bfloat16).at[0, : 3 * shift.shape[0]].set(
        split3(shift)
    )
    every = lax.all_gather(
        jnp.concatenate([whitened, shift_row], axis=0), "grp", axis=0, tiled=False
    )
    shift_grp = join3(every[:, local_cols, : 3 * shift.shape[0]]).reshape(groups, NPAN, window)
    every = jnp.transpose(every[:, :local_cols], (1, 0, 2)).reshape(groups, NPAN, window, total)

    panel_shift_row = jnp.zeros((1, total), jnp.bfloat16).at[0, : 3 * groups * window].set(
        split3(shift_grp[:, 0].reshape(-1))
    )
    panel_w = jnp.concatenate([every[:, 0].reshape(groups * window, total), panel_shift_row], 0)
    panel_w = lax.all_to_all(
        jnp.broadcast_to(panel_w[None], (colcount,) + panel_w.shape), "col", 0, 0, tiled=False
    )
    panel_w = lax.all_gather(panel_w, "row", axis=0, tiled=False)
    every, panel_w = lax.optimization_barrier((every, panel_w))
    shift_panel = join3(panel_w[:, :, groups * window, : 3 * groups * window])
    shift_panel = jnp.transpose(
        shift_panel.reshape(rowcount, colcount, groups, window), (2, 0, 1, 3)
    ).reshape(PW)
    panel_w = panel_w[:, :, : groups * window].reshape(rowcount, colcount, groups, window, total)
    panel_w = jnp.transpose(panel_w, (2, 0, 1, 3, 4)).reshape(PW, total)

    row_w = lax.dynamic_index_in_dim(every, group_index, 0, keepdims=False)
    row_w = lax.all_gather(row_w, "col", axis=0, tiled=False)
    row_w = jnp.transpose(row_w, (1, 0, 2, 3)).reshape(NPAN * colcount * window, total)

    col_w = lax.all_gather(every, "row", axis=0, tiled=False)
    col_w = jnp.transpose(col_w, (2, 1, 0, 3, 4)).reshape(NPAN * owners * window, total)

    panel_ids = jnp.arange(NPAN, dtype=jnp.int32)
    slab_ids = jnp.arange(slab, dtype=jnp.int32)
    owner_ids = jnp.arange(owners, dtype=jnp.int32)
    window_ids = jnp.arange(window, dtype=jnp.int32)
    own_owner = group_index * rowcount + row_index
    row_global = ((panel_ids[:, None] * owners + own_owner) * slab + slab_ids[None, :]).reshape(-1)
    col_global = (
        (panel_ids[:, None, None] * owners + owner_ids[None, :, None]) * slab
        + col_index * window
        + window_ids[None, None, :]
    ).reshape(-1)
    panel_ids_all = jnp.arange(PW, dtype=jnp.int32)
    shift_col = jnp.broadcast_to(
        shift.reshape(NPAN, 1, window), (NPAN, owners, window)
    ).reshape(-1)

    dims = (((1,), (1,)), ((), ()))
    f32 = jnp.float32
    diag_block = lax.dot_general(panel_w, panel_w, dims, preferred_element_type=f32)
    diag_block = diag_block + jnp.where(
        panel_ids_all[:, None] == panel_ids_all[None, :], shift_panel[None, :], 0.0
    )
    both_w = jnp.concatenate([row_w, col_w], axis=0)
    both_global = jnp.concatenate([row_global, col_global], axis=0)
    both_panel = lax.dot_general(both_w, panel_w, dims, preferred_element_type=f32)
    both_panel = both_panel + jnp.where(
        both_global[:, None] == panel_ids_all[None, :], shift_panel[None, :], 0.0
    )
    schur_tile = lax.dot_general(row_w, col_w, dims, preferred_element_type=f32)
    schur_tile = schur_tile + jnp.where(
        row_global[:, None] == col_global[None, :], shift_col[None, :], 0.0
    )

    inverse_factor_panel = inverse_cholesky(diag_block)
    solved = lax.dot_general(
        both_panel, inverse_factor_panel, dims, precision=highest, preferred_element_type=f32
    )
    local_rows = row_global.shape[0]
    row_factor = solved[:local_rows]
    col_factor = solved[local_rows:]

    panel_piece = lax.dynamic_slice_in_dim(
        row_factor.reshape(local_rows, owners, slab), col_index * window, window, 2
    ).reshape(local_rows, owners * window)
    panel_cols_global = col_global.reshape(NPAN, -1)[0]
    finished = jnp.where(row_global[:, None] >= panel_cols_global[None, :], panel_piece, 0.0)

    boundary = PANELS * PW
    first_trailing = owners * window
    update = jnp.dot(
        row_factor, col_factor[first_trailing:].T, precision=highest, preferred_element_type=f32
    )
    trailing = schur_tile[:, first_trailing:] - update
    trailing = jnp.where(row_global[:, None] >= boundary, trailing, 0.0)
    return jnp.concatenate([finished, trailing], axis=1)


def solution(mesh):
    in_specs = (
        P("grp", None, ("row", "col")),
        P("grp", None, None),
        P("grp"),
        P(("grp", "row", "col")),
    )
    out_specs = P(("grp", "row"), "col")
    return jax.shard_map(local, mesh=mesh, in_specs=in_specs, out_specs=out_specs, check_vma=False)
```

```python
import functools

import jax
import jax.numpy as jnp
from jax import lax
from jax.experimental import pallas as pl
from jax.experimental.pallas import tpu as pltpu
from jax.sharding import PartitionSpec as P

PW = 1024
PANELS = 1
NPAN = 10
HI = lax.Precision.HIGHEST


def _base_inverse(s):
    b = s.shape[0]
    lane = lax.broadcasted_iota(jnp.int32, (b, b), 1)
    sub = lax.broadcasted_iota(jnp.int32, (b, b), 0)
    sub_col = lax.broadcasted_iota(jnp.int32, (b, 1), 0)
    lane_row = lax.broadcasted_iota(jnp.int32, (1, b), 1)
    eye = jnp.where(lane == sub, 1.0, 0.0).astype(jnp.float32)

    def step(j, carry):
        work, inv = carry
        col = jnp.sum(jnp.where(lane == j, work, 0.0), axis=1, keepdims=True)
        row = jnp.sum(jnp.where(sub == j, work, 0.0), axis=0, keepdims=True)
        pivot = jnp.sum(jnp.where(lane_row == j, row, 0.0), axis=1, keepdims=True)
        scale = lax.rsqrt(pivot)
        l_col = jnp.where(sub_col >= j, col * scale, 0.0)
        l_row = jnp.where(lane_row >= j, row * scale, 0.0)
        work = work - l_col * l_row
        inv_row = jnp.sum(jnp.where(sub == j, inv, 0.0), axis=0, keepdims=True)
        diag = pivot * scale
        u = jnp.where(sub_col == j, l_col - 1.0, l_col) / diag
        inv = inv - u * inv_row
        return work, inv

    _, inv = lax.fori_loop(0, b, step, (s, eye))
    return inv


def _kernel(a_ref, z_ref, *, n, b):
    z_ref[...] = jnp.zeros_like(z_ref)
    for k in range(n // b):
        lo = k * b
        s = a_ref[lo:lo + b, lo:lo + b]
        if k > 0:
            zk = z_ref[0:lo, 0:lo]
            left = lax.dot_general(a_ref[lo:lo + b, 0:lo], zk, (((1,), (1,)), ((), ())),
                                   precision=HI, preferred_element_type=jnp.float32)
            s = s - lax.dot_general(left, left, (((1,), (1,)), ((), ())),
                                    precision=HI, preferred_element_type=jnp.float32)
        d = _base_inverse(s)
        z_ref[lo:lo + b, lo:lo + b] = d
        if k > 0:
            t = jnp.dot(left, zk, precision=HI, preferred_element_type=jnp.float32)
            z_ref[lo:lo + b, 0:lo] = -jnp.dot(d, t, precision=HI, preferred_element_type=jnp.float32)


def inverse_cholesky(a, b=128):
    n = a.shape[0]
    return pl.pallas_call(
        functools.partial(_kernel, n=n, b=b),
        out_shape=jax.ShapeDtypeStruct((n, n), jnp.float32),
        in_specs=[pl.BlockSpec(memory_space=pltpu.VMEM)],
        out_specs=pl.BlockSpec(memory_space=pltpu.VMEM),
        compiler_params=pltpu.CompilerParams(vmem_limit_bytes=48 * 1024 * 1024),
        cost_estimate=pl.CostEstimate(
            flops=2 * n * n * n, transcendentals=n, bytes_accessed=8 * n * n
        ),
    )(a)


def split3(x):
    hi = lax.reduce_precision(x, exponent_bits=8, mantissa_bits=7)
    rest = x - hi
    mid = lax.reduce_precision(rest, exponent_bits=8, mantissa_bits=7)
    lo = rest - mid
    return jnp.concatenate([hi, mid, lo]).astype(jnp.bfloat16)


def join3(parts):
    parts = parts.astype(jnp.float32).reshape(parts.shape[:-1] + (3, -1))
    return (parts[..., 0, :] + parts[..., 1, :]) + parts[..., 2, :]


def local(block_rows, inverse_factor, live_rows, shift):
    highest = lax.Precision.HIGHEST
    high = lax.Precision.HIGH
    groups = lax.axis_size("grp")
    rowcount = lax.axis_size("row")
    colcount = lax.axis_size("col")
    owners = groups * rowcount
    slab = PW // owners
    window = slab // colcount
    group_index = lax.axis_index("grp")
    row_index = lax.axis_index("row")
    col_index = lax.axis_index("col")
    blocks, padded, local_cols = block_rows.shape
    stacked = blocks * padded
    total = stacked * groups

    ordinal = jnp.arange(padded, dtype=jnp.int32)
    live_mask = (ordinal[None, :] < live_rows[:, None]).astype(jnp.float32)
    masked_factor = inverse_factor * live_mask[:, :, None] * live_mask[:, None, :]
    whitened = jnp.einsum(
        "bij,bjm->mbi", masked_factor, block_rows.astype(jnp.float32), precision=highest
    )
    whitened = whitened.astype(jnp.bfloat16).reshape(local_cols, stacked)

    shift_row = jnp.zeros((1, stacked), jnp.bfloat16).at[0, : 3 * shift.shape[0]].set(
        split3(shift)
    )
    every = lax.all_gather(
        jnp.concatenate([whitened, shift_row], axis=0), "grp", axis=0, tiled=False
    )
    shift_grp = join3(every[:, local_cols, : 3 * shift.shape[0]]).reshape(groups, NPAN, window)
    every = jnp.transpose(every[:, :local_cols], (1, 0, 2)).reshape(groups, NPAN, window, total)

    panel_shift_row = jnp.zeros((1, total), jnp.bfloat16).at[0, : 3 * groups * window].set(
        split3(shift_grp[:, 0].reshape(-1))
    )
    panel_w = jnp.concatenate([every[:, 0].reshape(groups * window, total), panel_shift_row], 0)
    panel_w = lax.all_to_all(
        jnp.broadcast_to(panel_w[None], (rowcount * colcount,) + panel_w.shape),
        ("row", "col"),
        0,
        0,
        tiled=False,
    ).reshape((rowcount, colcount) + panel_w.shape)
    every, panel_w = lax.optimization_barrier((every, panel_w))
    shift_panel = join3(panel_w[:, :, groups * window, : 3 * groups * window])
    shift_panel = jnp.transpose(
        shift_panel.reshape(rowcount, colcount, groups, window), (2, 0, 1, 3)
    ).reshape(PW)
    panel_w = panel_w[:, :, : groups * window].reshape(rowcount, colcount, groups, window, total)
    panel_w = jnp.transpose(panel_w, (2, 0, 1, 3, 4)).reshape(PW, total)

    row_w = lax.dynamic_index_in_dim(every, group_index, 0, keepdims=False)
    row_w = lax.all_gather(row_w, "col", axis=0, tiled=False)
    row_w = jnp.transpose(row_w, (1, 0, 2, 3)).reshape(NPAN * colcount * window, total)

    col_w = lax.all_gather(every, "row", axis=0, tiled=False)
    col_w = jnp.transpose(col_w, (2, 1, 0, 3, 4)).reshape(NPAN * owners * window, total)

    panel_ids = jnp.arange(NPAN, dtype=jnp.int32)
    slab_ids = jnp.arange(slab, dtype=jnp.int32)
    owner_ids = jnp.arange(owners, dtype=jnp.int32)
    window_ids = jnp.arange(window, dtype=jnp.int32)
    own_owner = group_index * rowcount + row_index
    row_global = ((panel_ids[:, None] * owners + own_owner) * slab + slab_ids[None, :]).reshape(-1)
    col_global = (
        (panel_ids[:, None, None] * owners + owner_ids[None, :, None]) * slab
        + col_index * window
        + window_ids[None, None, :]
    ).reshape(-1)
    panel_ids_all = jnp.arange(PW, dtype=jnp.int32)
    shift_col = jnp.broadcast_to(
        shift.reshape(NPAN, 1, window), (NPAN, owners, window)
    ).reshape(-1)

    dims = (((1,), (1,)), ((), ()))
    f32 = jnp.float32
    diag_block = lax.dot_general(panel_w, panel_w, dims, preferred_element_type=f32)
    diag_block = diag_block + jnp.where(
        panel_ids_all[:, None] == panel_ids_all[None, :], shift_panel[None, :], 0.0
    )
    both_w = jnp.concatenate([row_w, col_w], axis=0)
    both_global = jnp.concatenate([row_global, col_global], axis=0)
    both_panel = lax.dot_general(both_w, panel_w, dims, preferred_element_type=f32)
    both_panel = both_panel + jnp.where(
        both_global[:, None] == panel_ids_all[None, :], shift_panel[None, :], 0.0
    )
    schur_tile = lax.dot_general(row_w, col_w, dims, preferred_element_type=f32)
    schur_tile = schur_tile + jnp.where(
        row_global[:, None] == col_global[None, :], shift_col[None, :], 0.0
    )

    inverse_factor_panel = inverse_cholesky(diag_block)
    solved = lax.dot_general(
        both_panel, inverse_factor_panel, dims, precision=high, preferred_element_type=f32
    )
    local_rows = row_global.shape[0]
    row_factor = solved[:local_rows]
    col_factor = solved[local_rows:]

    panel_piece = lax.dynamic_slice_in_dim(
        row_factor.reshape(local_rows, owners, slab), col_index * window, window, 2
    ).reshape(local_rows, owners * window)
    panel_cols_global = col_global.reshape(NPAN, -1)[0]
    finished = jnp.where(row_global[:, None] >= panel_cols_global[None, :], panel_piece, 0.0)

    boundary = PANELS * PW
    first_trailing = owners * window
    update = jnp.dot(
        row_factor, col_factor[first_trailing:].T, precision=high, preferred_element_type=f32
    )
    trailing = schur_tile[:, first_trailing:] - update
    trailing = jnp.where(row_global[:, None] >= boundary, trailing, 0.0)
    return jnp.concatenate([finished, trailing], axis=1)


def solution(mesh):
    in_specs = (
        P("grp", None, ("row", "col")),
        P("grp", None, None),
        P("grp"),
        P(("grp", "row", "col")),
    )
    out_specs = P(("grp", "row"), "col")
    return jax.shard_map(local, mesh=mesh, in_specs=in_specs, out_specs=out_specs, check_vma=False)
```

```python
import functools

import jax
import jax.numpy as jnp
from jax import lax
from jax.experimental import pallas as pl
from jax.experimental.pallas import tpu as pltpu
from jax.sharding import PartitionSpec as P

PW = 1024
PANELS = 1
NPAN = 10
HI = lax.Precision.HIGHEST
MESH = pl.DeviceIdType.MESH


def _gather_kernel(x_ref, out_ref, local_sem, send_sem, recv_sem, *, axis, count):
    me = lax.axis_index(axis)
    barrier = pltpu.get_barrier_semaphore()
    for step in range(1, count):
        peer = lax.rem(me + step, count)
        pl.semaphore_signal(barrier, inc=1, device_id={axis: peer}, device_id_type=MESH)
    pl.semaphore_wait(barrier, count - 1)
    own = pltpu.make_async_copy(x_ref, out_ref.at[me], local_sem)
    own.start()
    copies = []
    for step in range(1, count):
        peer = lax.rem(me + step, count)
        copy = pltpu.make_async_remote_copy(
            src_ref=x_ref,
            dst_ref=out_ref.at[me],
            send_sem=send_sem.at[step],
            recv_sem=recv_sem.at[step],
            device_id={axis: peer},
            device_id_type=MESH,
        )
        copy.start()
        copies.append(copy)
    own.wait()
    for copy in copies:
        copy.wait()


def remote_gather(x, axis, count, collective_id):
    return pl.pallas_call(
        functools.partial(_gather_kernel, axis=axis, count=count),
        out_shape=jax.ShapeDtypeStruct((count,) + x.shape, x.dtype),
        in_specs=[pl.BlockSpec(memory_space=pl.ANY)],
        out_specs=pl.BlockSpec(memory_space=pl.ANY),
        scratch_shapes=[
            pltpu.SemaphoreType.DMA(()),
            pltpu.SemaphoreType.DMA((count,)),
            pltpu.SemaphoreType.DMA((count,)),
        ],
        compiler_params=pltpu.CompilerParams(collective_id=collective_id, has_side_effects=True),
    )(x)


def _base_inverse(s):
    b = s.shape[0]
    lane = lax.broadcasted_iota(jnp.int32, (b, b), 1)
    sub = lax.broadcasted_iota(jnp.int32, (b, b), 0)
    sub_col = lax.broadcasted_iota(jnp.int32, (b, 1), 0)
    lane_row = lax.broadcasted_iota(jnp.int32, (1, b), 1)
    eye = jnp.where(lane == sub, 1.0, 0.0).astype(jnp.float32)

    def step(j, carry):
        work, inv = carry
        col = jnp.sum(jnp.where(lane == j, work, 0.0), axis=1, keepdims=True)
        row = jnp.sum(jnp.where(sub == j, work, 0.0), axis=0, keepdims=True)
        pivot = jnp.sum(jnp.where(lane_row == j, row, 0.0), axis=1, keepdims=True)
        scale = lax.rsqrt(pivot)
        l_col = jnp.where(sub_col >= j, col * scale, 0.0)
        l_row = jnp.where(lane_row >= j, row * scale, 0.0)
        work = work - l_col * l_row
        inv_row = jnp.sum(jnp.where(sub == j, inv, 0.0), axis=0, keepdims=True)
        diag = pivot * scale
        u = jnp.where(sub_col == j, l_col - 1.0, l_col) / diag
        inv = inv - u * inv_row
        return work, inv

    _, inv = lax.fori_loop(0, b, step, (s, eye))
    return inv


def _kernel(a_ref, z_ref, *, n, b):
    z_ref[...] = jnp.zeros_like(z_ref)
    for k in range(n // b):
        lo = k * b
        s = a_ref[lo:lo + b, lo:lo + b]
        if k > 0:
            zk = z_ref[0:lo, 0:lo]
            left = lax.dot_general(a_ref[lo:lo + b, 0:lo], zk, (((1,), (1,)), ((), ())),
                                   precision=HI, preferred_element_type=jnp.float32)
            s = s - lax.dot_general(left, left, (((1,), (1,)), ((), ())),
                                    precision=HI, preferred_element_type=jnp.float32)
        d = _base_inverse(s)
        z_ref[lo:lo + b, lo:lo + b] = d
        if k > 0:
            t = jnp.dot(left, zk, precision=HI, preferred_element_type=jnp.float32)
            z_ref[lo:lo + b, 0:lo] = -jnp.dot(d, t, precision=HI, preferred_element_type=jnp.float32)


def inverse_cholesky(a, b=128):
    n = a.shape[0]
    return pl.pallas_call(
        functools.partial(_kernel, n=n, b=b),
        out_shape=jax.ShapeDtypeStruct((n, n), jnp.float32),
        in_specs=[pl.BlockSpec(memory_space=pltpu.VMEM)],
        out_specs=pl.BlockSpec(memory_space=pltpu.VMEM),
        compiler_params=pltpu.CompilerParams(vmem_limit_bytes=48 * 1024 * 1024),
        cost_estimate=pl.CostEstimate(
            flops=2 * n * n * n, transcendentals=n, bytes_accessed=8 * n * n
        ),
    )(a)


def split3(x):
    hi = lax.reduce_precision(x, exponent_bits=8, mantissa_bits=7)
    rest = x - hi
    mid = lax.reduce_precision(rest, exponent_bits=8, mantissa_bits=7)
    lo = rest - mid
    return jnp.concatenate([hi, mid, lo]).astype(jnp.bfloat16)


def join3(parts):
    parts = parts.astype(jnp.float32).reshape(parts.shape[:-1] + (3, -1))
    return (parts[..., 0, :] + parts[..., 1, :]) + parts[..., 2, :]


def local(block_rows, inverse_factor, live_rows, shift):
    highest = lax.Precision.HIGHEST
    high = lax.Precision.HIGH
    groups = lax.axis_size("grp")
    rowcount = lax.axis_size("row")
    colcount = lax.axis_size("col")
    owners = groups * rowcount
    slab = PW // owners
    window = slab // colcount
    group_index = lax.axis_index("grp")
    row_index = lax.axis_index("row")
    col_index = lax.axis_index("col")
    blocks, padded, local_cols = block_rows.shape
    stacked = blocks * padded
    total = stacked * groups

    ordinal = jnp.arange(padded, dtype=jnp.int32)
    live_mask = (ordinal[None, :] < live_rows[:, None]).astype(jnp.float32)
    masked_factor = inverse_factor * live_mask[:, :, None] * live_mask[:, None, :]
    whitened = jnp.einsum(
        "bij,bjm->mbi", masked_factor, block_rows.astype(jnp.float32), precision=highest
    )
    whitened = whitened.astype(jnp.bfloat16).reshape(local_cols, stacked)

    shift_row = jnp.zeros((1, stacked), jnp.bfloat16).at[0, : 3 * shift.shape[0]].set(
        split3(shift)
    )
    every = lax.all_gather(
        jnp.concatenate([whitened, shift_row], axis=0), "grp", axis=0, tiled=False
    )
    shift_grp = join3(every[:, local_cols, : 3 * shift.shape[0]]).reshape(groups, NPAN, window)
    every = jnp.transpose(every[:, :local_cols], (1, 0, 2)).reshape(groups, NPAN, window, total)

    panel_shift_row = jnp.zeros((1, total), jnp.bfloat16).at[0, : 3 * groups * window].set(
        split3(shift_grp[:, 0].reshape(-1))
    )
    panel_w = jnp.concatenate([every[:, 0].reshape(groups * window, total), panel_shift_row], 0)
    panel_w = remote_gather(panel_w, "col", colcount, 0)
    panel_w = remote_gather(panel_w, "row", rowcount, 1)
    every, panel_w = lax.optimization_barrier((every, panel_w))
    shift_panel = join3(panel_w[:, :, groups * window, : 3 * groups * window])
    shift_panel = jnp.transpose(
        shift_panel.reshape(rowcount, colcount, groups, window), (2, 0, 1, 3)
    ).reshape(PW)
    panel_w = panel_w[:, :, : groups * window].reshape(rowcount, colcount, groups, window, total)
    panel_w = jnp.transpose(panel_w, (2, 0, 1, 3, 4)).reshape(PW, total)

    row_w = lax.dynamic_index_in_dim(every, group_index, 0, keepdims=False)
    row_w = lax.all_gather(row_w, "col", axis=0, tiled=False)
    row_w = jnp.transpose(row_w, (1, 0, 2, 3)).reshape(NPAN * colcount * window, total)

    col_w = lax.all_gather(every, "row", axis=0, tiled=False)
    col_w = jnp.transpose(col_w, (2, 1, 0, 3, 4)).reshape(NPAN * owners * window, total)

    panel_ids = jnp.arange(NPAN, dtype=jnp.int32)
    slab_ids = jnp.arange(slab, dtype=jnp.int32)
    owner_ids = jnp.arange(owners, dtype=jnp.int32)
    window_ids = jnp.arange(window, dtype=jnp.int32)
    own_owner = group_index * rowcount + row_index
    row_global = ((panel_ids[:, None] * owners + own_owner) * slab + slab_ids[None, :]).reshape(-1)
    col_global = (
        (panel_ids[:, None, None] * owners + owner_ids[None, :, None]) * slab
        + col_index * window
        + window_ids[None, None, :]
    ).reshape(-1)
    panel_ids_all = jnp.arange(PW, dtype=jnp.int32)
    shift_col = jnp.broadcast_to(
        shift.reshape(NPAN, 1, window), (NPAN, owners, window)
    ).reshape(-1)

    dims = (((1,), (1,)), ((), ()))
    f32 = jnp.float32
    diag_block = lax.dot_general(panel_w, panel_w, dims, preferred_element_type=f32)
    diag_block = diag_block + jnp.where(
        panel_ids_all[:, None] == panel_ids_all[None, :], shift_panel[None, :], 0.0
    )
    both_w = jnp.concatenate([row_w, col_w], axis=0)
    both_global = jnp.concatenate([row_global, col_global], axis=0)
    both_panel = lax.dot_general(both_w, panel_w, dims, preferred_element_type=f32)
    both_panel = both_panel + jnp.where(
        both_global[:, None] == panel_ids_all[None, :], shift_panel[None, :], 0.0
    )
    schur_tile = lax.dot_general(row_w, col_w, dims, preferred_element_type=f32)
    schur_tile = schur_tile + jnp.where(
        row_global[:, None] == col_global[None, :], shift_col[None, :], 0.0
    )

    inverse_factor_panel = inverse_cholesky(diag_block)
    solved = lax.dot_general(
        both_panel, inverse_factor_panel, dims, precision=high, preferred_element_type=f32
    )
    local_rows = row_global.shape[0]
    row_factor = solved[:local_rows]
    col_factor = solved[local_rows:]

    panel_piece = lax.dynamic_slice_in_dim(
        row_factor.reshape(local_rows, owners, slab), col_index * window, window, 2
    ).reshape(local_rows, owners * window)
    panel_cols_global = col_global.reshape(NPAN, -1)[0]
    finished = jnp.where(row_global[:, None] >= panel_cols_global[None, :], panel_piece, 0.0)

    boundary = PANELS * PW
    first_trailing = owners * window
    update = jnp.dot(
        row_factor, col_factor[first_trailing:].T, precision=high, preferred_element_type=f32
    )
    trailing = schur_tile[:, first_trailing:] - update
    trailing = jnp.where(row_global[:, None] >= boundary, trailing, 0.0)
    return jnp.concatenate([finished, trailing], axis=1)


def solution(mesh):
    in_specs = (
        P("grp", None, ("row", "col")),
        P("grp", None, None),
        P("grp"),
        P(("grp", "row", "col")),
    )
    out_specs = P(("grp", "row"), "col")
    return jax.shard_map(local, mesh=mesh, in_specs=in_specs, out_specs=out_specs, check_vma=False)
```

```python
import functools

import jax
import jax.numpy as jnp
from jax import lax
from jax.experimental import pallas as pl
from jax.experimental.pallas import tpu as pltpu
from jax.sharding import PartitionSpec as P

PW = 1024
PANELS = 1
NPAN = 10
HI = lax.Precision.HIGHEST
MESH = pl.DeviceIdType.MESH


def _gather_kernel(x_ref, out_ref, local_sem, send_sem, recv_sem, *, axis, count):
    me = lax.axis_index(axis)
    barrier = pltpu.get_barrier_semaphore()
    for step in range(1, count):
        peer = lax.rem(me + step, count)
        pl.semaphore_signal(barrier, inc=1, device_id={axis: peer}, device_id_type=MESH)
    pl.semaphore_wait(barrier, count - 1)
    own = pltpu.make_async_copy(x_ref, out_ref.at[me], local_sem)
    own.start()
    copies = []
    for step in range(1, count):
        peer = lax.rem(me + step, count)
        copy = pltpu.make_async_remote_copy(
            src_ref=x_ref,
            dst_ref=out_ref.at[me],
            send_sem=send_sem.at[step],
            recv_sem=recv_sem.at[step],
            device_id={axis: peer},
            device_id_type=MESH,
        )
        copy.start()
        copies.append(copy)
    own.wait()
    for copy in copies:
        copy.wait()


def remote_gather(x, axis, count, collective_id):
    return pl.pallas_call(
        functools.partial(_gather_kernel, axis=axis, count=count),
        out_shape=jax.ShapeDtypeStruct((count,) + x.shape, x.dtype),
        in_specs=[pl.BlockSpec(memory_space=pl.ANY)],
        out_specs=pl.BlockSpec(memory_space=pl.ANY),
        scratch_shapes=[
            pltpu.SemaphoreType.DMA(()),
            pltpu.SemaphoreType.DMA((count,)),
            pltpu.SemaphoreType.DMA((count,)),
        ],
        compiler_params=pltpu.CompilerParams(collective_id=collective_id, has_side_effects=True),
    )(x)


def _base_inverse(s):
    b = s.shape[0]
    lane = lax.broadcasted_iota(jnp.int32, (b, b), 1)
    sub = lax.broadcasted_iota(jnp.int32, (b, b), 0)
    sub_col = lax.broadcasted_iota(jnp.int32, (b, 1), 0)
    lane_row = lax.broadcasted_iota(jnp.int32, (1, b), 1)
    eye = jnp.where(lane == sub, 1.0, 0.0).astype(jnp.float32)

    def step(i, carry):
        work, inv = carry
        j = 2 * i
        k = j + 1
        row_a = jnp.sum(jnp.where(sub == j, work, 0.0), axis=0, keepdims=True)
        row_b = jnp.sum(jnp.where(sub == k, work, 0.0), axis=0, keepdims=True)
        col_a = jnp.sum(jnp.where(lane == j, work, 0.0), axis=1, keepdims=True)
        col_b = jnp.sum(jnp.where(lane == k, work, 0.0), axis=1, keepdims=True)
        piv_a = jnp.sum(jnp.where(lane_row == j, row_a, 0.0), axis=1, keepdims=True)
        off = jnp.sum(jnp.where(lane_row == k, row_a, 0.0), axis=1, keepdims=True)
        piv_b = jnp.sum(jnp.where(lane_row == k, row_b, 0.0), axis=1, keepdims=True)
        scale_a = lax.rsqrt(piv_a)
        below = off * scale_a
        scale_b = lax.rsqrt(piv_b - below * below)
        la_col = jnp.where(sub_col >= j, col_a * scale_a, 0.0)
        la_row = jnp.where(lane_row >= j, row_a * scale_a, 0.0)
        lb_col = jnp.where(sub_col >= k, (col_b - la_col * below) * scale_b, 0.0)
        lb_row = jnp.where(lane_row >= k, (row_b - la_row * below) * scale_b, 0.0)
        work = work - la_col * la_row - lb_col * lb_row
        inv_a = jnp.sum(jnp.where(sub == j, inv, 0.0), axis=0, keepdims=True)
        inv_b = jnp.sum(jnp.where(sub == k, inv, 0.0), axis=0, keepdims=True)
        inv_b = inv_b - (below * scale_a) * inv_a
        ua = jnp.where(sub_col == j, la_col - 1.0, la_col) * scale_a
        ub = jnp.where(sub_col == k, lb_col - 1.0, lb_col) * scale_b
        inv = inv - ua * inv_a - ub * inv_b
        return work, inv

    _, inv = lax.fori_loop(0, b // 2, step, (s, eye))
    return inv


def _kernel(a_ref, z_ref, *, n, b):
    z_ref[...] = jnp.zeros_like(z_ref)
    for k in range(n // b):
        lo = k * b
        s = a_ref[lo:lo + b, lo:lo + b]
        if k > 0:
            zk = z_ref[0:lo, 0:lo]
            left = lax.dot_general(a_ref[lo:lo + b, 0:lo], zk, (((1,), (1,)), ((), ())),
                                   precision=HI, preferred_element_type=jnp.float32)
            s = s - lax.dot_general(left, left, (((1,), (1,)), ((), ())),
                                    precision=HI, preferred_element_type=jnp.float32)
        d = _base_inverse(s)
        z_ref[lo:lo + b, lo:lo + b] = d
        if k > 0:
            t = jnp.dot(left, zk, precision=HI, preferred_element_type=jnp.float32)
            z_ref[lo:lo + b, 0:lo] = -jnp.dot(d, t, precision=HI, preferred_element_type=jnp.float32)


def inverse_cholesky(a, b=128):
    n = a.shape[0]
    return pl.pallas_call(
        functools.partial(_kernel, n=n, b=b),
        out_shape=jax.ShapeDtypeStruct((n, n), jnp.float32),
        in_specs=[pl.BlockSpec(memory_space=pltpu.VMEM)],
        out_specs=pl.BlockSpec(memory_space=pltpu.VMEM),
        compiler_params=pltpu.CompilerParams(vmem_limit_bytes=48 * 1024 * 1024),
        cost_estimate=pl.CostEstimate(
            flops=2 * n * n * n, transcendentals=n, bytes_accessed=8 * n * n
        ),
    )(a)


def split3(x):
    hi = lax.reduce_precision(x, exponent_bits=8, mantissa_bits=7)
    rest = x - hi
    mid = lax.reduce_precision(rest, exponent_bits=8, mantissa_bits=7)
    lo = rest - mid
    return jnp.concatenate([hi, mid, lo]).astype(jnp.bfloat16)


def join3(parts):
    parts = parts.astype(jnp.float32).reshape(parts.shape[:-1] + (3, -1))
    return (parts[..., 0, :] + parts[..., 1, :]) + parts[..., 2, :]


def local(block_rows, inverse_factor, live_rows, shift):
    highest = lax.Precision.HIGHEST
    high = lax.Precision.HIGH
    groups = lax.axis_size("grp")
    rowcount = lax.axis_size("row")
    colcount = lax.axis_size("col")
    owners = groups * rowcount
    slab = PW // owners
    window = slab // colcount
    group_index = lax.axis_index("grp")
    row_index = lax.axis_index("row")
    col_index = lax.axis_index("col")
    blocks, padded, local_cols = block_rows.shape
    stacked = blocks * padded
    total = stacked * groups

    ordinal = jnp.arange(padded, dtype=jnp.int32)
    live_mask = (ordinal[None, :] < live_rows[:, None]).astype(jnp.float32)
    masked_factor = inverse_factor * live_mask[:, :, None] * live_mask[:, None, :]
    whitened = jnp.einsum(
        "bij,bjm->mbi", masked_factor, block_rows.astype(jnp.float32), precision=highest
    )
    whitened = whitened.astype(jnp.bfloat16).reshape(local_cols, stacked)

    shift_row = jnp.zeros((1, stacked), jnp.bfloat16).at[0, : 3 * shift.shape[0]].set(
        split3(shift)
    )
    every = lax.all_gather(
        jnp.concatenate([whitened, shift_row], axis=0), "grp", axis=0, tiled=False
    )
    shift_grp = join3(every[:, local_cols, : 3 * shift.shape[0]]).reshape(groups, NPAN, window)
    every = jnp.transpose(every[:, :local_cols], (1, 0, 2)).reshape(groups, NPAN, window, total)

    panel_shift_row = jnp.zeros((1, total), jnp.bfloat16).at[0, : 3 * groups * window].set(
        split3(shift_grp[:, 0].reshape(-1))
    )
    panel_w = jnp.concatenate([every[:, 0].reshape(groups * window, total), panel_shift_row], 0)
    panel_w = remote_gather(panel_w, "col", colcount, 0)
    panel_w = lax.all_gather(panel_w, "row", axis=0, tiled=False)
    every, panel_w = lax.optimization_barrier((every, panel_w))
    shift_panel = join3(panel_w[:, :, groups * window, : 3 * groups * window])
    shift_panel = jnp.transpose(
        shift_panel.reshape(rowcount, colcount, groups, window), (2, 0, 1, 3)
    ).reshape(PW)
    panel_w = panel_w[:, :, : groups * window].reshape(rowcount, colcount, groups, window, total)
    panel_w = jnp.transpose(panel_w, (2, 0, 1, 3, 4)).reshape(PW, total)

    row_w = lax.dynamic_index_in_dim(every, group_index, 0, keepdims=False)
    row_w = lax.all_gather(row_w, "col", axis=0, tiled=False)
    row_w = jnp.transpose(row_w, (1, 0, 2, 3)).reshape(NPAN * colcount * window, total)

    col_w = lax.all_gather(every, "row", axis=0, tiled=False)
    col_w = jnp.transpose(col_w, (2, 1, 0, 3, 4)).reshape(NPAN * owners * window, total)

    panel_ids = jnp.arange(NPAN, dtype=jnp.int32)
    slab_ids = jnp.arange(slab, dtype=jnp.int32)
    owner_ids = jnp.arange(owners, dtype=jnp.int32)
    window_ids = jnp.arange(window, dtype=jnp.int32)
    own_owner = group_index * rowcount + row_index
    row_global = ((panel_ids[:, None] * owners + own_owner) * slab + slab_ids[None, :]).reshape(-1)
    col_global = (
        (panel_ids[:, None, None] * owners + owner_ids[None, :, None]) * slab
        + col_index * window
        + window_ids[None, None, :]
    ).reshape(-1)
    panel_ids_all = jnp.arange(PW, dtype=jnp.int32)
    shift_col = jnp.broadcast_to(
        shift.reshape(NPAN, 1, window), (NPAN, owners, window)
    ).reshape(-1)

    dims = (((1,), (1,)), ((), ()))
    f32 = jnp.float32
    diag_block = lax.dot_general(panel_w, panel_w, dims, preferred_element_type=f32)
    diag_block = diag_block + jnp.where(
        panel_ids_all[:, None] == panel_ids_all[None, :], shift_panel[None, :], 0.0
    )
    both_w = jnp.concatenate([row_w, col_w], axis=0)
    both_global = jnp.concatenate([row_global, col_global], axis=0)
    both_panel = lax.dot_general(both_w, panel_w, dims, preferred_element_type=f32)
    both_panel = both_panel + jnp.where(
        both_global[:, None] == panel_ids_all[None, :], shift_panel[None, :], 0.0
    )
    schur_tile = lax.dot_general(row_w, col_w, dims, preferred_element_type=f32)
    schur_tile = schur_tile + jnp.where(
        row_global[:, None] == col_global[None, :], shift_col[None, :], 0.0
    )

    inverse_factor_panel = inverse_cholesky(diag_block)
    solved = lax.dot_general(
        both_panel, inverse_factor_panel, dims, precision=high, preferred_element_type=f32
    )
    local_rows = row_global.shape[0]
    row_factor = solved[:local_rows]
    col_factor = solved[local_rows:]

    panel_piece = lax.dynamic_slice_in_dim(
        row_factor.reshape(local_rows, owners, slab), col_index * window, window, 2
    ).reshape(local_rows, owners * window)
    panel_cols_global = col_global.reshape(NPAN, -1)[0]
    finished = jnp.where(row_global[:, None] >= panel_cols_global[None, :], panel_piece, 0.0)

    boundary = PANELS * PW
    first_trailing = owners * window
    update = jnp.dot(
        row_factor, col_factor[first_trailing:].T, precision=high, preferred_element_type=f32
    )
    trailing = schur_tile[:, first_trailing:] - update
    trailing = jnp.where(row_global[:, None] >= boundary, trailing, 0.0)
    return jnp.concatenate([finished, trailing], axis=1)


def solution(mesh):
    in_specs = (
        P("grp", None, ("row", "col")),
        P("grp", None, None),
        P("grp"),
        P(("grp", "row", "col")),
    )
    out_specs = P(("grp", "row"), "col")
    return jax.shard_map(local, mesh=mesh, in_specs=in_specs, out_specs=out_specs, check_vma=False)
```

```python
import functools

import jax
import jax.numpy as jnp
from jax import lax
from jax.experimental import pallas as pl
from jax.experimental.pallas import tpu as pltpu
from jax.sharding import PartitionSpec as P

PW = 1024
PANELS = 1
NPAN = 10
HI = lax.Precision.HIGHEST
MESH = pl.DeviceIdType.MESH


def _gather_kernel(x_ref, out_ref, local_sem, send_sem, recv_sem, *, axis, count):
    me = lax.axis_index(axis)
    barrier = pltpu.get_barrier_semaphore()
    for step in range(1, count):
        peer = lax.rem(me + step, count)
        pl.semaphore_signal(barrier, inc=1, device_id={axis: peer}, device_id_type=MESH)
    pl.semaphore_wait(barrier, count - 1)
    own = pltpu.make_async_copy(x_ref, out_ref.at[me], local_sem)
    own.start()
    copies = []
    for step in range(1, count):
        peer = lax.rem(me + step, count)
        copy = pltpu.make_async_remote_copy(
            src_ref=x_ref,
            dst_ref=out_ref.at[me],
            send_sem=send_sem.at[step],
            recv_sem=recv_sem.at[step],
            device_id={axis: peer},
            device_id_type=MESH,
        )
        copy.start()
        copies.append(copy)
    own.wait()
    for copy in copies:
        copy.wait()


def remote_gather(x, axis, count, collective_id):
    return pl.pallas_call(
        functools.partial(_gather_kernel, axis=axis, count=count),
        out_shape=jax.ShapeDtypeStruct((count,) + x.shape, x.dtype),
        in_specs=[pl.BlockSpec(memory_space=pl.ANY)],
        out_specs=pl.BlockSpec(memory_space=pl.ANY),
        scratch_shapes=[
            pltpu.SemaphoreType.DMA(()),
            pltpu.SemaphoreType.DMA((count,)),
            pltpu.SemaphoreType.DMA((count,)),
        ],
        compiler_params=pltpu.CompilerParams(collective_id=collective_id, has_side_effects=True),
    )(x)


def _base_inverse(s):
    b = s.shape[0]
    lane = lax.broadcasted_iota(jnp.int32, (b, b), 1)
    sub = lax.broadcasted_iota(jnp.int32, (b, b), 0)
    sub_col = lax.broadcasted_iota(jnp.int32, (b, 1), 0)
    lane_row = lax.broadcasted_iota(jnp.int32, (1, b), 1)
    eye = jnp.where(lane == sub, 1.0, 0.0).astype(jnp.float32)

    width = 4

    def step(i, carry):
        work, inv = carry
        first = width * i
        rows = [jnp.sum(jnp.where(sub == first + q, work, 0.0), axis=0, keepdims=True)
                for q in range(width)]
        cols = [jnp.sum(jnp.where(lane == first + q, work, 0.0), axis=1, keepdims=True)
                for q in range(width)]
        invs = [jnp.sum(jnp.where(sub == first + q, inv, 0.0), axis=0, keepdims=True)
                for q in range(width)]
        block = [[jnp.sum(jnp.where(lane_row == first + r, rows[q], 0.0), axis=1, keepdims=True)
                  for r in range(width)] for q in range(width)]
        small = [[None] * width for _ in range(width)]
        scales = []
        for q in range(width):
            for p in range(q):
                acc = block[p][q]
                for t in range(p):
                    acc = acc - small[q][t] * small[p][t]
                small[q][p] = acc * scales[p]
            d = block[q][q]
            for t in range(q):
                d = d - small[q][t] * small[q][t]
            scales.append(lax.rsqrt(d))
        lcols, lrows, xrows = [], [], []
        for q in range(width):
            c, r, x = cols[q], rows[q], invs[q]
            for p in range(q):
                c = c - lcols[p] * small[q][p]
                r = r - lrows[p] * small[q][p]
                x = x - (small[q][p] * scales[p]) * xrows[p]
            lcols.append(jnp.where(sub_col >= first + q, c * scales[q], 0.0))
            lrows.append(jnp.where(lane_row >= first + q, r * scales[q], 0.0))
            xrows.append(x)
        for q in range(width):
            work = work - lcols[q] * lrows[q]
            u = jnp.where(sub_col == first + q, lcols[q] - 1.0, lcols[q]) * scales[q]
            inv = inv - u * xrows[q]
        return work, inv

    _, inv = lax.fori_loop(0, b // width, step, (s, eye))
    return inv


def _kernel(a_ref, z_ref, *, n, b):
    z_ref[...] = jnp.zeros_like(z_ref)
    for k in range(n // b):
        lo = k * b
        s = a_ref[lo:lo + b, lo:lo + b]
        if k > 0:
            zk = z_ref[0:lo, 0:lo]
            left = lax.dot_general(a_ref[lo:lo + b, 0:lo], zk, (((1,), (1,)), ((), ())),
                                   precision=HI, preferred_element_type=jnp.float32)
            s = s - lax.dot_general(left, left, (((1,), (1,)), ((), ())),
                                    precision=HI, preferred_element_type=jnp.float32)
        d = _base_inverse(s)
        z_ref[lo:lo + b, lo:lo + b] = d
        if k > 0:
            t = jnp.dot(left, zk, precision=HI, preferred_element_type=jnp.float32)
            z_ref[lo:lo + b, 0:lo] = -jnp.dot(d, t, precision=HI, preferred_element_type=jnp.float32)


def inverse_cholesky(a, b=128):
    n = a.shape[0]
    return pl.pallas_call(
        functools.partial(_kernel, n=n, b=b),
        out_shape=jax.ShapeDtypeStruct((n, n), jnp.float32),
        in_specs=[pl.BlockSpec(memory_space=pltpu.VMEM)],
        out_specs=pl.BlockSpec(memory_space=pltpu.VMEM),
        compiler_params=pltpu.CompilerParams(vmem_limit_bytes=48 * 1024 * 1024),
        cost_estimate=pl.CostEstimate(
            flops=2 * n * n * n, transcendentals=n, bytes_accessed=8 * n * n
        ),
    )(a)


def split3(x):
    hi = lax.reduce_precision(x, exponent_bits=8, mantissa_bits=7)
    rest = x - hi
    mid = lax.reduce_precision(rest, exponent_bits=8, mantissa_bits=7)
    lo = rest - mid
    return jnp.concatenate([hi, mid, lo]).astype(jnp.bfloat16)


def join3(parts):
    parts = parts.astype(jnp.float32).reshape(parts.shape[:-1] + (3, -1))
    return (parts[..., 0, :] + parts[..., 1, :]) + parts[..., 2, :]


def local(block_rows, inverse_factor, live_rows, shift):
    highest = lax.Precision.HIGHEST
    high = lax.Precision.HIGH
    groups = lax.axis_size("grp")
    rowcount = lax.axis_size("row")
    colcount = lax.axis_size("col")
    owners = groups * rowcount
    slab = PW // owners
    window = slab // colcount
    group_index = lax.axis_index("grp")
    row_index = lax.axis_index("row")
    col_index = lax.axis_index("col")
    blocks, padded, local_cols = block_rows.shape
    stacked = blocks * padded
    total = stacked * groups

    ordinal = jnp.arange(padded, dtype=jnp.int32)
    live_mask = (ordinal[None, :] < live_rows[:, None]).astype(jnp.float32)
    masked_factor = inverse_factor * live_mask[:, :, None] * live_mask[:, None, :]
    whitened = jnp.einsum(
        "bij,bjm->mbi", masked_factor, block_rows.astype(jnp.float32), precision=highest
    )
    whitened = whitened.astype(jnp.bfloat16).reshape(local_cols, stacked)

    shift_row = jnp.zeros((1, stacked), jnp.bfloat16).at[0, : 3 * shift.shape[0]].set(
        split3(shift)
    )
    every = lax.all_gather(
        jnp.concatenate([whitened, shift_row], axis=0), "grp", axis=0, tiled=False
    )
    shift_grp = join3(every[:, local_cols, : 3 * shift.shape[0]]).reshape(groups, NPAN, window)
    every = jnp.transpose(every[:, :local_cols], (1, 0, 2)).reshape(groups, NPAN, window, total)

    panel_shift_row = jnp.zeros((1, total), jnp.bfloat16).at[0, : 3 * groups * window].set(
        split3(shift_grp[:, 0].reshape(-1))
    )
    panel_w = jnp.concatenate([every[:, 0].reshape(groups * window, total), panel_shift_row], 0)
    panel_w = remote_gather(panel_w, "col", colcount, 0)
    panel_w = lax.all_gather(panel_w, "row", axis=0, tiled=False)
    every, panel_w = lax.optimization_barrier((every, panel_w))
    shift_panel = join3(panel_w[:, :, groups * window, : 3 * groups * window])
    shift_panel = jnp.transpose(
        shift_panel.reshape(rowcount, colcount, groups, window), (2, 0, 1, 3)
    ).reshape(PW)
    panel_w = panel_w[:, :, : groups * window].reshape(rowcount, colcount, groups, window, total)
    panel_w = jnp.transpose(panel_w, (2, 0, 1, 3, 4)).reshape(PW, total)

    row_w = lax.dynamic_index_in_dim(every, group_index, 0, keepdims=False)
    row_w = lax.all_gather(row_w, "col", axis=0, tiled=False)
    row_w = jnp.transpose(row_w, (1, 0, 2, 3)).reshape(NPAN * colcount * window, total)

    col_w = lax.all_gather(every, "row", axis=0, tiled=False)
    col_w = jnp.transpose(col_w, (2, 1, 0, 3, 4)).reshape(NPAN * owners * window, total)

    panel_ids = jnp.arange(NPAN, dtype=jnp.int32)
    slab_ids = jnp.arange(slab, dtype=jnp.int32)
    owner_ids = jnp.arange(owners, dtype=jnp.int32)
    window_ids = jnp.arange(window, dtype=jnp.int32)
    own_owner = group_index * rowcount + row_index
    row_global = ((panel_ids[:, None] * owners + own_owner) * slab + slab_ids[None, :]).reshape(-1)
    col_global = (
        (panel_ids[:, None, None] * owners + owner_ids[None, :, None]) * slab
        + col_index * window
        + window_ids[None, None, :]
    ).reshape(-1)
    panel_ids_all = jnp.arange(PW, dtype=jnp.int32)
    shift_col = jnp.broadcast_to(
        shift.reshape(NPAN, 1, window), (NPAN, owners, window)
    ).reshape(-1)

    dims = (((1,), (1,)), ((), ()))
    f32 = jnp.float32
    diag_block = lax.dot_general(panel_w, panel_w, dims, preferred_element_type=f32)
    diag_block = diag_block + jnp.where(
        panel_ids_all[:, None] == panel_ids_all[None, :], shift_panel[None, :], 0.0
    )
    both_w = jnp.concatenate([row_w, col_w], axis=0)
    both_global = jnp.concatenate([row_global, col_global], axis=0)
    both_panel = lax.dot_general(both_w, panel_w, dims, preferred_element_type=f32)
    both_panel = both_panel + jnp.where(
        both_global[:, None] == panel_ids_all[None, :], shift_panel[None, :], 0.0
    )
    schur_tile = lax.dot_general(row_w, col_w, dims, preferred_element_type=f32)
    schur_tile = schur_tile + jnp.where(
        row_global[:, None] == col_global[None, :], shift_col[None, :], 0.0
    )

    inverse_factor_panel = inverse_cholesky(diag_block)
    solved = lax.dot_general(
        both_panel, inverse_factor_panel, dims, precision=high, preferred_element_type=f32
    )
    local_rows = row_global.shape[0]
    row_factor = solved[:local_rows]
    col_factor = solved[local_rows:]

    panel_piece = lax.dynamic_slice_in_dim(
        row_factor.reshape(local_rows, owners, slab), col_index * window, window, 2
    ).reshape(local_rows, owners * window)
    panel_cols_global = col_global.reshape(NPAN, -1)[0]
    finished = jnp.where(row_global[:, None] >= panel_cols_global[None, :], panel_piece, 0.0)

    boundary = PANELS * PW
    first_trailing = owners * window
    update = jnp.dot(
        row_factor, col_factor[first_trailing:].T, precision=high, preferred_element_type=f32
    )
    trailing = schur_tile[:, first_trailing:] - update
    trailing = jnp.where(row_global[:, None] >= boundary, trailing, 0.0)
    return jnp.concatenate([finished, trailing], axis=1)


def solution(mesh):
    in_specs = (
        P("grp", None, ("row", "col")),
        P("grp", None, None),
        P("grp"),
        P(("grp", "row", "col")),
    )
    out_specs = P(("grp", "row"), "col")
    return jax.shard_map(local, mesh=mesh, in_specs=in_specs, out_specs=out_specs, check_vma=False)
```

```python
import functools

import jax
import jax.numpy as jnp
from jax import lax
from jax.experimental import pallas as pl
from jax.experimental.pallas import tpu as pltpu
from jax.sharding import PartitionSpec as P

PW = 1024
PANELS = 1
NPAN = 10
HI = lax.Precision.HIGHEST
MESH = pl.DeviceIdType.MESH


def _gather_kernel(x_ref, out_ref, local_sem, send_sem, recv_sem, *, axis, count):
    me = lax.axis_index(axis)
    barrier = pltpu.get_barrier_semaphore()
    for step in range(1, count):
        peer = lax.rem(me + step, count)
        pl.semaphore_signal(barrier, inc=1, device_id={axis: peer}, device_id_type=MESH)
    pl.semaphore_wait(barrier, count - 1)
    own = pltpu.make_async_copy(x_ref, out_ref.at[me], local_sem)
    own.start()
    copies = []
    for step in range(1, count):
        peer = lax.rem(me + step, count)
        copy = pltpu.make_async_remote_copy(
            src_ref=x_ref,
            dst_ref=out_ref.at[me],
            send_sem=send_sem.at[step],
            recv_sem=recv_sem.at[step],
            device_id={axis: peer},
            device_id_type=MESH,
        )
        copy.start()
        copies.append(copy)
    own.wait()
    for copy in copies:
        copy.wait()


def remote_gather(x, axis, count, collective_id):
    return pl.pallas_call(
        functools.partial(_gather_kernel, axis=axis, count=count),
        out_shape=jax.ShapeDtypeStruct((count,) + x.shape, x.dtype),
        in_specs=[pl.BlockSpec(memory_space=pl.ANY)],
        out_specs=pl.BlockSpec(memory_space=pl.ANY),
        scratch_shapes=[
            pltpu.SemaphoreType.DMA(()),
            pltpu.SemaphoreType.DMA((count,)),
            pltpu.SemaphoreType.DMA((count,)),
        ],
        compiler_params=pltpu.CompilerParams(collective_id=collective_id, has_side_effects=True),
    )(x)


def _base_inverse(s):
    b = s.shape[0]
    lane = lax.broadcasted_iota(jnp.int32, (b, b), 1)
    sub = lax.broadcasted_iota(jnp.int32, (b, b), 0)
    sub_col = lax.broadcasted_iota(jnp.int32, (b, 1), 0)
    lane_row = lax.broadcasted_iota(jnp.int32, (1, b), 1)
    eye = jnp.where(lane == sub, 1.0, 0.0).astype(jnp.float32)

    width = 4

    def step(i, carry):
        work, inv = carry
        first = width * i
        rows = [jnp.sum(jnp.where(sub == first + q, work, 0.0), axis=0, keepdims=True)
                for q in range(width)]
        cols = [jnp.sum(jnp.where(lane == first + q, work, 0.0), axis=1, keepdims=True)
                for q in range(width)]
        invs = [jnp.sum(jnp.where(sub == first + q, inv, 0.0), axis=0, keepdims=True)
                for q in range(width)]
        block = [[jnp.sum(jnp.where(lane_row == first + r, rows[q], 0.0), axis=1, keepdims=True)
                  for r in range(width)] for q in range(width)]
        small = [[None] * width for _ in range(width)]
        scales = []
        for q in range(width):
            for p in range(q):
                acc = block[p][q]
                for t in range(p):
                    acc = acc - small[q][t] * small[p][t]
                small[q][p] = acc * scales[p]
            d = block[q][q]
            for t in range(q):
                d = d - small[q][t] * small[q][t]
            scales.append(lax.rsqrt(d))
        lcols, lrows, xrows = [], [], []
        for q in range(width):
            c, r, x = cols[q], rows[q], invs[q]
            for p in range(q):
                c = c - lcols[p] * small[q][p]
                r = r - lrows[p] * small[q][p]
                x = x - (small[q][p] * scales[p]) * xrows[p]
            lcols.append(jnp.where(sub_col >= first + q, c * scales[q], 0.0))
            lrows.append(jnp.where(lane_row >= first + q, r * scales[q], 0.0))
            xrows.append(x)
        for q in range(width):
            work = work - lcols[q] * lrows[q]
            u = jnp.where(sub_col == first + q, lcols[q] - 1.0, lcols[q]) * scales[q]
            inv = inv - u * xrows[q]
        return work, inv

    _, inv = lax.fori_loop(0, b // width, step, (s, eye))
    return inv


def _kernel(a_ref, z_ref, *, n, b):
    z_ref[...] = jnp.zeros_like(z_ref)
    for k in range(n // b):
        lo = k * b
        s = a_ref[lo:lo + b, lo:lo + b]
        if k > 0:
            zk = z_ref[0:lo, 0:lo]
            left = lax.dot_general(a_ref[lo:lo + b, 0:lo], zk, (((1,), (1,)), ((), ())),
                                   precision=HI, preferred_element_type=jnp.float32)
            s = s - lax.dot_general(left, left, (((1,), (1,)), ((), ())),
                                    precision=HI, preferred_element_type=jnp.float32)
        d = _base_inverse(s)
        z_ref[lo:lo + b, lo:lo + b] = d
        if k > 0:
            t = jnp.dot(left, zk, precision=HI, preferred_element_type=jnp.float32)
            z_ref[lo:lo + b, 0:lo] = -jnp.dot(d, t, precision=HI, preferred_element_type=jnp.float32)


def inverse_cholesky(a, b=128):
    n = a.shape[0]
    return pl.pallas_call(
        functools.partial(_kernel, n=n, b=b),
        out_shape=jax.ShapeDtypeStruct((n, n), jnp.float32),
        in_specs=[pl.BlockSpec(memory_space=pltpu.VMEM)],
        out_specs=pl.BlockSpec(memory_space=pltpu.VMEM),
        compiler_params=pltpu.CompilerParams(vmem_limit_bytes=48 * 1024 * 1024),
        cost_estimate=pl.CostEstimate(
            flops=2 * n * n * n, transcendentals=n, bytes_accessed=8 * n * n
        ),
    )(a)


def split3(x):
    hi = lax.reduce_precision(x, exponent_bits=8, mantissa_bits=7)
    rest = x - hi
    mid = lax.reduce_precision(rest, exponent_bits=8, mantissa_bits=7)
    lo = rest - mid
    return jnp.concatenate([hi, mid, lo]).astype(jnp.bfloat16)


def join3(parts):
    parts = parts.astype(jnp.float32).reshape(parts.shape[:-1] + (3, -1))
    return (parts[..., 0, :] + parts[..., 1, :]) + parts[..., 2, :]


def local(block_rows, inverse_factor, live_rows, shift):
    highest = lax.Precision.HIGHEST
    high = lax.Precision.HIGH
    groups = lax.axis_size("grp")
    rowcount = lax.axis_size("row")
    colcount = lax.axis_size("col")
    owners = groups * rowcount
    slab = PW // owners
    window = slab // colcount
    group_index = lax.axis_index("grp")
    row_index = lax.axis_index("row")
    col_index = lax.axis_index("col")
    blocks, padded, local_cols = block_rows.shape
    stacked = blocks * padded
    total = stacked * groups

    ordinal = jnp.arange(padded, dtype=jnp.int32)
    live_mask = (ordinal[None, :] < live_rows[:, None]).astype(jnp.float32)
    masked_factor = inverse_factor * live_mask[:, :, None] * live_mask[:, None, :]
    whitened = jnp.einsum(
        "bij,bjm->mbi", masked_factor, block_rows.astype(jnp.float32), precision=highest
    )
    whitened = whitened.astype(jnp.bfloat16).reshape(local_cols, stacked)

    shift_row = jnp.zeros((1, stacked), jnp.bfloat16).at[0, : 3 * shift.shape[0]].set(
        split3(shift)
    )
    every = lax.all_gather(
        jnp.concatenate([whitened, shift_row], axis=0), "grp", axis=0, tiled=False
    )
    shift_grp = join3(every[:, local_cols, : 3 * shift.shape[0]]).reshape(groups, NPAN, window)
    every = jnp.transpose(every[:, :local_cols], (1, 0, 2)).reshape(groups, NPAN, window, total)

    panel_shift_row = jnp.zeros((1, total), jnp.bfloat16).at[0, : 3 * groups * window].set(
        split3(shift_grp[:, 0].reshape(-1))
    )
    panel_w = jnp.concatenate([every[:, 0].reshape(groups * window, total), panel_shift_row], 0)
    col_w = lax.all_gather(every, "row", axis=0, tiled=False)
    panel_w = remote_gather(panel_w, "col", colcount, 0)
    panel_w, col_w = lax.optimization_barrier((panel_w, col_w))
    panel_w = lax.all_gather(panel_w, "row", axis=0, tiled=False)
    every, panel_w = lax.optimization_barrier((every, panel_w))
    shift_panel = join3(panel_w[:, :, groups * window, : 3 * groups * window])
    shift_panel = jnp.transpose(
        shift_panel.reshape(rowcount, colcount, groups, window), (2, 0, 1, 3)
    ).reshape(PW)
    panel_w = panel_w[:, :, : groups * window].reshape(rowcount, colcount, groups, window, total)
    panel_w = jnp.transpose(panel_w, (2, 0, 1, 3, 4)).reshape(PW, total)

    row_w = lax.dynamic_index_in_dim(every, group_index, 0, keepdims=False)
    row_w = lax.all_gather(row_w, "col", axis=0, tiled=False)
    row_w = jnp.transpose(row_w, (1, 0, 2, 3)).reshape(NPAN * colcount * window, total)

    col_w = jnp.transpose(col_w, (2, 1, 0, 3, 4)).reshape(NPAN * owners * window, total)

    panel_ids = jnp.arange(NPAN, dtype=jnp.int32)
    slab_ids = jnp.arange(slab, dtype=jnp.int32)
    owner_ids = jnp.arange(owners, dtype=jnp.int32)
    window_ids = jnp.arange(window, dtype=jnp.int32)
    own_owner = group_index * rowcount + row_index
    row_global = ((panel_ids[:, None] * owners + own_owner) * slab + slab_ids[None, :]).reshape(-1)
    col_global = (
        (panel_ids[:, None, None] * owners + owner_ids[None, :, None]) * slab
        + col_index * window
        + window_ids[None, None, :]
    ).reshape(-1)
    panel_ids_all = jnp.arange(PW, dtype=jnp.int32)
    shift_col = jnp.broadcast_to(
        shift.reshape(NPAN, 1, window), (NPAN, owners, window)
    ).reshape(-1)

    dims = (((1,), (1,)), ((), ()))
    f32 = jnp.float32
    diag_block = lax.dot_general(panel_w, panel_w, dims, preferred_element_type=f32)
    diag_block = diag_block + jnp.where(
        panel_ids_all[:, None] == panel_ids_all[None, :], shift_panel[None, :], 0.0
    )
    both_w = jnp.concatenate([row_w, col_w], axis=0)
    both_global = jnp.concatenate([row_global, col_global], axis=0)
    both_panel = lax.dot_general(both_w, panel_w, dims, preferred_element_type=f32)
    both_panel = both_panel + jnp.where(
        both_global[:, None] == panel_ids_all[None, :], shift_panel[None, :], 0.0
    )
    schur_tile = lax.dot_general(row_w, col_w, dims, preferred_element_type=f32)
    schur_tile = schur_tile + jnp.where(
        row_global[:, None] == col_global[None, :], shift_col[None, :], 0.0
    )

    inverse_factor_panel = inverse_cholesky(diag_block)
    solved = lax.dot_general(
        both_panel, inverse_factor_panel, dims, precision=high, preferred_element_type=f32
    )
    local_rows = row_global.shape[0]
    row_factor = solved[:local_rows]
    col_factor = solved[local_rows:]

    panel_piece = lax.dynamic_slice_in_dim(
        row_factor.reshape(local_rows, owners, slab), col_index * window, window, 2
    ).reshape(local_rows, owners * window)
    panel_cols_global = col_global.reshape(NPAN, -1)[0]
    finished = jnp.where(row_global[:, None] >= panel_cols_global[None, :], panel_piece, 0.0)

    boundary = PANELS * PW
    first_trailing = owners * window
    update = jnp.dot(
        row_factor, col_factor[first_trailing:].T, precision=high, preferred_element_type=f32
    )
    trailing = schur_tile[:, first_trailing:] - update
    trailing = jnp.where(row_global[:, None] >= boundary, trailing, 0.0)
    return jnp.concatenate([finished, trailing], axis=1)


def solution(mesh):
    in_specs = (
        P("grp", None, ("row", "col")),
        P("grp", None, None),
        P("grp"),
        P(("grp", "row", "col")),
    )
    out_specs = P(("grp", "row"), "col")
    return jax.shard_map(local, mesh=mesh, in_specs=in_specs, out_specs=out_specs, check_vma=False)
```

```python
import functools

import jax
import jax.numpy as jnp
from jax import lax
from jax.experimental import pallas as pl
from jax.experimental.pallas import tpu as pltpu
from jax.sharding import PartitionSpec as P

PW = 1024
PANELS = 1
NPAN = 10
HI = lax.Precision.HIGH
MESH = pl.DeviceIdType.MESH


def _gather_kernel(x_ref, out_ref, local_sem, send_sem, recv_sem, *, axis, count):
    me = lax.axis_index(axis)
    barrier = pltpu.get_barrier_semaphore()
    for step in range(1, count):
        peer = lax.rem(me + step, count)
        pl.semaphore_signal(barrier, inc=1, device_id={axis: peer}, device_id_type=MESH)
    pl.semaphore_wait(barrier, count - 1)
    own = pltpu.make_async_copy(x_ref, out_ref.at[me], local_sem)
    own.start()
    copies = []
    for step in range(1, count):
        peer = lax.rem(me + step, count)
        copy = pltpu.make_async_remote_copy(
            src_ref=x_ref,
            dst_ref=out_ref.at[me],
            send_sem=send_sem.at[step],
            recv_sem=recv_sem.at[step],
            device_id={axis: peer},
            device_id_type=MESH,
        )
        copy.start()
        copies.append(copy)
    own.wait()
    for copy in copies:
        copy.wait()


def remote_gather(x, axis, count, collective_id):
    return pl.pallas_call(
        functools.partial(_gather_kernel, axis=axis, count=count),
        out_shape=jax.ShapeDtypeStruct((count,) + x.shape, x.dtype),
        in_specs=[pl.BlockSpec(memory_space=pl.ANY)],
        out_specs=pl.BlockSpec(memory_space=pl.ANY),
        scratch_shapes=[
            pltpu.SemaphoreType.DMA(()),
            pltpu.SemaphoreType.DMA((count,)),
            pltpu.SemaphoreType.DMA((count,)),
        ],
        compiler_params=pltpu.CompilerParams(collective_id=collective_id, has_side_effects=True),
    )(x)


def _base_inverse(s):
    b = s.shape[0]
    lane = lax.broadcasted_iota(jnp.int32, (b, b), 1)
    sub = lax.broadcasted_iota(jnp.int32, (b, b), 0)
    sub_col = lax.broadcasted_iota(jnp.int32, (b, 1), 0)
    lane_row = lax.broadcasted_iota(jnp.int32, (1, b), 1)
    eye = jnp.where(lane == sub, 1.0, 0.0).astype(jnp.float32)

    width = 4

    def step(i, carry):
        work, inv = carry
        first = width * i
        rows = [jnp.sum(jnp.where(sub == first + q, work, 0.0), axis=0, keepdims=True)
                for q in range(width)]
        cols = [jnp.sum(jnp.where(lane == first + q, work, 0.0), axis=1, keepdims=True)
                for q in range(width)]
        invs = [jnp.sum(jnp.where(sub == first + q, inv, 0.0), axis=0, keepdims=True)
                for q in range(width)]
        block = [[jnp.sum(jnp.where(lane_row == first + r, rows[q], 0.0), axis=1, keepdims=True)
                  for r in range(width)] for q in range(width)]
        small = [[None] * width for _ in range(width)]
        scales = []
        for q in range(width):
            for p in range(q):
                acc = block[p][q]
                for t in range(p):
                    acc = acc - small[q][t] * small[p][t]
                small[q][p] = acc * scales[p]
            d = block[q][q]
            for t in range(q):
                d = d - small[q][t] * small[q][t]
            scales.append(lax.rsqrt(d))
        lcols, lrows, xrows = [], [], []
        for q in range(width):
            c, r, x = cols[q], rows[q], invs[q]
            for p in range(q):
                c = c - lcols[p] * small[q][p]
                r = r - lrows[p] * small[q][p]
                x = x - (small[q][p] * scales[p]) * xrows[p]
            lcols.append(jnp.where(sub_col >= first + q, c * scales[q], 0.0))
            lrows.append(jnp.where(lane_row >= first + q, r * scales[q], 0.0))
            xrows.append(x)
        for q in range(width):
            work = work - lcols[q] * lrows[q]
            u = jnp.where(sub_col == first + q, lcols[q] - 1.0, lcols[q]) * scales[q]
            inv = inv - u * xrows[q]
        return work, inv

    _, inv = lax.fori_loop(0, b // width, step, (s, eye))
    return inv


def _kernel(a_ref, z_ref, *, n, b):
    z_ref[...] = jnp.zeros_like(z_ref)
    for k in range(n // b):
        lo = k * b
        s = a_ref[lo:lo + b, lo:lo + b]
        if k > 0:
            zk = z_ref[0:lo, 0:lo]
            left = lax.dot_general(a_ref[lo:lo + b, 0:lo], zk, (((1,), (1,)), ((), ())),
                                   precision=HI, preferred_element_type=jnp.float32)
            s = s - lax.dot_general(left, left, (((1,), (1,)), ((), ())),
                                    precision=HI, preferred_element_type=jnp.float32)
        d = _base_inverse(s)
        z_ref[lo:lo + b, lo:lo + b] = d
        if k > 0:
            t = jnp.dot(left, zk, precision=HI, preferred_element_type=jnp.float32)
            z_ref[lo:lo + b, 0:lo] = -jnp.dot(d, t, precision=HI, preferred_element_type=jnp.float32)


def inverse_cholesky(a, b=128):
    n = a.shape[0]
    return pl.pallas_call(
        functools.partial(_kernel, n=n, b=b),
        out_shape=jax.ShapeDtypeStruct((n, n), jnp.float32),
        in_specs=[pl.BlockSpec(memory_space=pltpu.VMEM)],
        out_specs=pl.BlockSpec(memory_space=pltpu.VMEM),
        compiler_params=pltpu.CompilerParams(vmem_limit_bytes=48 * 1024 * 1024),
        cost_estimate=pl.CostEstimate(
            flops=2 * n * n * n, transcendentals=n, bytes_accessed=8 * n * n
        ),
    )(a)


def split3(x):
    hi = lax.reduce_precision(x, exponent_bits=8, mantissa_bits=7)
    rest = x - hi
    mid = lax.reduce_precision(rest, exponent_bits=8, mantissa_bits=7)
    lo = rest - mid
    return jnp.concatenate([hi, mid, lo]).astype(jnp.bfloat16)


def join3(parts):
    parts = parts.astype(jnp.float32).reshape(parts.shape[:-1] + (3, -1))
    return (parts[..., 0, :] + parts[..., 1, :]) + parts[..., 2, :]


def local(block_rows, inverse_factor, live_rows, shift):
    highest = lax.Precision.HIGHEST
    high = lax.Precision.HIGH
    groups = lax.axis_size("grp")
    rowcount = lax.axis_size("row")
    colcount = lax.axis_size("col")
    owners = groups * rowcount
    slab = PW // owners
    window = slab // colcount
    group_index = lax.axis_index("grp")
    row_index = lax.axis_index("row")
    col_index = lax.axis_index("col")
    blocks, padded, local_cols = block_rows.shape
    stacked = blocks * padded
    total = stacked * groups

    ordinal = jnp.arange(padded, dtype=jnp.int32)
    live_mask = (ordinal[None, :] < live_rows[:, None]).astype(jnp.float32)
    masked_factor = inverse_factor * live_mask[:, :, None] * live_mask[:, None, :]
    whitened = jnp.einsum(
        "bij,bjm->mbi", masked_factor, block_rows.astype(jnp.float32), precision=highest
    )
    whitened = whitened.astype(jnp.bfloat16).reshape(local_cols, stacked)

    shift_row = jnp.zeros((1, stacked), jnp.bfloat16).at[0, : 3 * shift.shape[0]].set(
        split3(shift)
    )
    every = lax.all_gather(
        jnp.concatenate([whitened, shift_row], axis=0), "grp", axis=0, tiled=False
    )
    shift_grp = join3(every[:, local_cols, : 3 * shift.shape[0]]).reshape(groups, NPAN, window)
    every = jnp.transpose(every[:, :local_cols], (1, 0, 2)).reshape(groups, NPAN, window, total)

    panel_shift_row = jnp.zeros((1, total), jnp.bfloat16).at[0, : 3 * groups * window].set(
        split3(shift_grp[:, 0].reshape(-1))
    )
    panel_w = jnp.concatenate([every[:, 0].reshape(groups * window, total), panel_shift_row], 0)
    col_w = lax.all_gather(every, "row", axis=0, tiled=False)
    panel_w = remote_gather(panel_w, "col", colcount, 0)
    panel_w, col_w = lax.optimization_barrier((panel_w, col_w))
    panel_w = lax.all_gather(panel_w, "row", axis=0, tiled=False)
    every, panel_w = lax.optimization_barrier((every, panel_w))
    shift_panel = join3(panel_w[:, :, groups * window, : 3 * groups * window])
    shift_panel = jnp.transpose(
        shift_panel.reshape(rowcount, colcount, groups, window), (2, 0, 1, 3)
    ).reshape(PW)
    panel_w = panel_w[:, :, : groups * window].reshape(rowcount, colcount, groups, window, total)
    panel_w = jnp.transpose(panel_w, (2, 0, 1, 3, 4)).reshape(PW, total)

    row_w = lax.dynamic_index_in_dim(every, group_index, 0, keepdims=False)
    row_w = lax.all_gather(row_w, "col", axis=0, tiled=False)
    row_w = jnp.transpose(row_w, (1, 0, 2, 3)).reshape(NPAN * colcount * window, total)

    col_w = jnp.transpose(col_w, (2, 1, 0, 3, 4)).reshape(NPAN * owners * window, total)

    panel_ids = jnp.arange(NPAN, dtype=jnp.int32)
    slab_ids = jnp.arange(slab, dtype=jnp.int32)
    owner_ids = jnp.arange(owners, dtype=jnp.int32)
    window_ids = jnp.arange(window, dtype=jnp.int32)
    own_owner = group_index * rowcount + row_index
    row_global = ((panel_ids[:, None] * owners + own_owner) * slab + slab_ids[None, :]).reshape(-1)
    col_global = (
        (panel_ids[:, None, None] * owners + owner_ids[None, :, None]) * slab
        + col_index * window
        + window_ids[None, None, :]
    ).reshape(-1)
    panel_ids_all = jnp.arange(PW, dtype=jnp.int32)
    shift_col = jnp.broadcast_to(
        shift.reshape(NPAN, 1, window), (NPAN, owners, window)
    ).reshape(-1)

    dims = (((1,), (1,)), ((), ()))
    f32 = jnp.float32
    diag_block = lax.dot_general(panel_w, panel_w, dims, preferred_element_type=f32)
    diag_block = diag_block + jnp.where(
        panel_ids_all[:, None] == panel_ids_all[None, :], shift_panel[None, :], 0.0
    )
    both_w = jnp.concatenate([row_w, col_w], axis=0)
    both_global = jnp.concatenate([row_global, col_global], axis=0)
    both_panel = lax.dot_general(both_w, panel_w, dims, preferred_element_type=f32)
    both_panel = both_panel + jnp.where(
        both_global[:, None] == panel_ids_all[None, :], shift_panel[None, :], 0.0
    )
    schur_tile = lax.dot_general(row_w, col_w, dims, preferred_element_type=f32)
    schur_tile = schur_tile + jnp.where(
        row_global[:, None] == col_global[None, :], shift_col[None, :], 0.0
    )

    inverse_factor_panel = inverse_cholesky(diag_block)
    solved = lax.dot_general(
        both_panel, inverse_factor_panel, dims, precision=high, preferred_element_type=f32
    )
    local_rows = row_global.shape[0]
    row_factor = solved[:local_rows]
    col_factor = solved[local_rows:]

    panel_piece = lax.dynamic_slice_in_dim(
        row_factor.reshape(local_rows, owners, slab), col_index * window, window, 2
    ).reshape(local_rows, owners * window)
    panel_cols_global = col_global.reshape(NPAN, -1)[0]
    finished = jnp.where(row_global[:, None] >= panel_cols_global[None, :], panel_piece, 0.0)

    boundary = PANELS * PW
    first_trailing = owners * window
    update = jnp.dot(
        row_factor, col_factor[first_trailing:].T, precision=high, preferred_element_type=f32
    )
    trailing = schur_tile[:, first_trailing:] - update
    trailing = jnp.where(row_global[:, None] >= boundary, trailing, 0.0)
    return jnp.concatenate([finished, trailing], axis=1)


def solution(mesh):
    in_specs = (
        P("grp", None, ("row", "col")),
        P("grp", None, None),
        P("grp"),
        P(("grp", "row", "col")),
    )
    out_specs = P(("grp", "row"), "col")
    return jax.shard_map(local, mesh=mesh, in_specs=in_specs, out_specs=out_specs, check_vma=False)
```

```python
import functools

import jax
import jax.numpy as jnp
from jax import lax
from jax.experimental import pallas as pl
from jax.experimental.pallas import tpu as pltpu
from jax.sharding import PartitionSpec as P

PW = 1024
PANELS = 1
NPAN = 10
HI = lax.Precision.HIGH
MESH = pl.DeviceIdType.MESH


def _gather_kernel(x_ref, out_ref, local_sem, send_sem, recv_sem, *, axis, count, position):
    me = lax.axis_index(axis)
    slot = out_ref.at[(slice(None),) * position + (me,)]
    barrier = pltpu.get_barrier_semaphore()
    for step in range(1, count):
        peer = lax.rem(me + step, count)
        pl.semaphore_signal(barrier, inc=1, device_id={axis: peer}, device_id_type=MESH)
    pl.semaphore_wait(barrier, count - 1)
    own = pltpu.make_async_copy(x_ref, slot, local_sem)
    own.start()
    copies = []
    for step in range(1, count):
        peer = lax.rem(me + step, count)
        copy = pltpu.make_async_remote_copy(
            src_ref=x_ref,
            dst_ref=slot,
            send_sem=send_sem.at[step],
            recv_sem=recv_sem.at[step],
            device_id={axis: peer},
            device_id_type=MESH,
        )
        copy.start()
        copies.append(copy)
    own.wait()
    for copy in copies:
        copy.wait()


def remote_gather(x, axis, count, collective_id, position=0):
    return pl.pallas_call(
        functools.partial(_gather_kernel, axis=axis, count=count, position=position),
        out_shape=jax.ShapeDtypeStruct(
            x.shape[:position] + (count,) + x.shape[position:], x.dtype
        ),
        in_specs=[pl.BlockSpec(memory_space=pl.ANY)],
        out_specs=pl.BlockSpec(memory_space=pl.ANY),
        scratch_shapes=[
            pltpu.SemaphoreType.DMA(()),
            pltpu.SemaphoreType.DMA((count,)),
            pltpu.SemaphoreType.DMA((count,)),
        ],
        compiler_params=pltpu.CompilerParams(collective_id=collective_id, has_side_effects=True),
    )(x)


def _base_inverse(s):
    b = s.shape[0]
    lane = lax.broadcasted_iota(jnp.int32, (b, b), 1)
    sub = lax.broadcasted_iota(jnp.int32, (b, b), 0)
    sub_col = lax.broadcasted_iota(jnp.int32, (b, 1), 0)
    lane_row = lax.broadcasted_iota(jnp.int32, (1, b), 1)
    eye = jnp.where(lane == sub, 1.0, 0.0).astype(jnp.float32)

    width = 4

    def step(i, carry):
        work, inv = carry
        first = width * i
        rows = [jnp.sum(jnp.where(sub == first + q, work, 0.0), axis=0, keepdims=True)
                for q in range(width)]
        cols = [jnp.sum(jnp.where(lane == first + q, work, 0.0), axis=1, keepdims=True)
                for q in range(width)]
        invs = [jnp.sum(jnp.where(sub == first + q, inv, 0.0), axis=0, keepdims=True)
                for q in range(width)]
        block = [[jnp.sum(jnp.where(lane_row == first + r, rows[q], 0.0), axis=1, keepdims=True)
                  for r in range(width)] for q in range(width)]
        small = [[None] * width for _ in range(width)]
        scales = []
        for q in range(width):
            for p in range(q):
                acc = block[p][q]
                for t in range(p):
                    acc = acc - small[q][t] * small[p][t]
                small[q][p] = acc * scales[p]
            d = block[q][q]
            for t in range(q):
                d = d - small[q][t] * small[q][t]
            scales.append(lax.rsqrt(d))
        lcols, lrows, xrows = [], [], []
        for q in range(width):
            c, r, x = cols[q], rows[q], invs[q]
            for p in range(q):
                c = c - lcols[p] * small[q][p]
                r = r - lrows[p] * small[q][p]
                x = x - (small[q][p] * scales[p]) * xrows[p]
            lcols.append(jnp.where(sub_col >= first + q, c * scales[q], 0.0))
            lrows.append(jnp.where(lane_row >= first + q, r * scales[q], 0.0))
            xrows.append(x)
        for q in range(width):
            work = work - lcols[q] * lrows[q]
            u = jnp.where(sub_col == first + q, lcols[q] - 1.0, lcols[q]) * scales[q]
            inv = inv - u * xrows[q]
        return work, inv

    _, inv = lax.fori_loop(0, b // width, step, (s, eye))
    return inv


def _kernel(a_ref, z_ref, *, n, b):
    z_ref[...] = jnp.zeros_like(z_ref)
    for k in range(n // b):
        lo = k * b
        s = a_ref[lo:lo + b, lo:lo + b]
        if k > 0:
            zk = z_ref[0:lo, 0:lo]
            left = lax.dot_general(a_ref[lo:lo + b, 0:lo], zk, (((1,), (1,)), ((), ())),
                                   precision=HI, preferred_element_type=jnp.float32)
            s = s - lax.dot_general(left, left, (((1,), (1,)), ((), ())),
                                    precision=HI, preferred_element_type=jnp.float32)
        d = _base_inverse(s)
        z_ref[lo:lo + b, lo:lo + b] = d
        if k > 0:
            t = jnp.dot(left, zk, precision=HI, preferred_element_type=jnp.float32)
            z_ref[lo:lo + b, 0:lo] = -jnp.dot(d, t, precision=HI, preferred_element_type=jnp.float32)


def inverse_cholesky(a, b=128):
    n = a.shape[0]
    return pl.pallas_call(
        functools.partial(_kernel, n=n, b=b),
        out_shape=jax.ShapeDtypeStruct((n, n), jnp.float32),
        in_specs=[pl.BlockSpec(memory_space=pltpu.VMEM)],
        out_specs=pl.BlockSpec(memory_space=pltpu.VMEM),
        compiler_params=pltpu.CompilerParams(vmem_limit_bytes=48 * 1024 * 1024),
        cost_estimate=pl.CostEstimate(
            flops=2 * n * n * n, transcendentals=n, bytes_accessed=8 * n * n
        ),
    )(a)


def split3(x):
    hi = lax.reduce_precision(x, exponent_bits=8, mantissa_bits=7)
    rest = x - hi
    mid = lax.reduce_precision(rest, exponent_bits=8, mantissa_bits=7)
    lo = rest - mid
    return jnp.concatenate([hi, mid, lo], axis=-1).astype(jnp.bfloat16)


def join3(parts):
    parts = parts.astype(jnp.float32).reshape(parts.shape[:-1] + (3, -1))
    return (parts[..., 0, :] + parts[..., 1, :]) + parts[..., 2, :]


def local(block_rows, inverse_factor, live_rows, shift):
    highest = lax.Precision.HIGHEST
    high = lax.Precision.HIGH
    groups = lax.axis_size("grp")
    rowcount = lax.axis_size("row")
    colcount = lax.axis_size("col")
    owners = groups * rowcount
    slab = PW // owners
    window = slab // colcount
    group_index = lax.axis_index("grp")
    row_index = lax.axis_index("row")
    col_index = lax.axis_index("col")
    blocks, padded, local_cols = block_rows.shape
    stacked = blocks * padded
    total = stacked * groups

    ordinal = jnp.arange(padded, dtype=jnp.int32)
    live_mask = (ordinal[None, :] < live_rows[:, None]).astype(jnp.float32)
    masked_factor = inverse_factor * live_mask[:, :, None] * live_mask[:, None, :]
    whitened = jnp.einsum(
        "bij,bjm->mbi", masked_factor, block_rows.astype(jnp.float32), precision=highest
    )
    whitened = whitened.astype(jnp.bfloat16).reshape(local_cols, stacked)

    shift_row = jnp.zeros((1, stacked), jnp.bfloat16).at[0, : 3 * shift.shape[0]].set(
        split3(shift)
    )
    every = lax.all_gather(
        jnp.concatenate([whitened, shift_row], axis=0), "grp", axis=0, tiled=False
    )
    shift_grp = join3(every[:, local_cols, : 3 * shift.shape[0]]).reshape(groups, NPAN, window)
    every = jnp.transpose(every[:, :local_cols], (1, 0, 2)).reshape(groups, NPAN, window, total)

    panel_shift_row = jnp.zeros((groups, 1, total), jnp.bfloat16).at[:, 0, : 3 * window].set(
        split3(shift_grp[:, 0])
    )
    panel_w = jnp.concatenate([every[:, 0], panel_shift_row], 1)
    col_w = lax.all_gather(every, "row", axis=0, tiled=False)
    panel_w = remote_gather(panel_w, "col", colcount, 0, position=1)
    panel_w, col_w = lax.optimization_barrier((panel_w, col_w))
    panel_w = lax.all_gather(panel_w, "row", axis=1, tiled=False)
    every, panel_w = lax.optimization_barrier((every, panel_w))
    shift_panel = join3(panel_w[:, :, :, window, : 3 * window]).reshape(PW)
    panel_w = panel_w[:, :, :, :window].reshape(PW, total)

    row_w = lax.dynamic_index_in_dim(every, group_index, 0, keepdims=False)
    row_w = lax.all_gather(row_w, "col", axis=0, tiled=False)
    row_w = jnp.transpose(row_w, (1, 0, 2, 3)).reshape(NPAN * colcount * window, total)

    col_w = jnp.transpose(col_w, (2, 1, 0, 3, 4)).reshape(NPAN * owners * window, total)

    panel_ids = jnp.arange(NPAN, dtype=jnp.int32)
    slab_ids = jnp.arange(slab, dtype=jnp.int32)
    owner_ids = jnp.arange(owners, dtype=jnp.int32)
    window_ids = jnp.arange(window, dtype=jnp.int32)
    own_owner = group_index * rowcount + row_index
    row_global = ((panel_ids[:, None] * owners + own_owner) * slab + slab_ids[None, :]).reshape(-1)
    col_global = (
        (panel_ids[:, None, None] * owners + owner_ids[None, :, None]) * slab
        + col_index * window
        + window_ids[None, None, :]
    ).reshape(-1)
    panel_ids_all = jnp.arange(PW, dtype=jnp.int32)
    shift_col = jnp.broadcast_to(
        shift.reshape(NPAN, 1, window), (NPAN, owners, window)
    ).reshape(-1)

    dims = (((1,), (1,)), ((), ()))
    f32 = jnp.float32
    diag_block = lax.dot_general(panel_w, panel_w, dims, preferred_element_type=f32)
    diag_block = diag_block + jnp.where(
        panel_ids_all[:, None] == panel_ids_all[None, :], shift_panel[None, :], 0.0
    )
    both_w = jnp.concatenate([row_w, col_w], axis=0)
    both_global = jnp.concatenate([row_global, col_global], axis=0)
    both_panel = lax.dot_general(both_w, panel_w, dims, preferred_element_type=f32)
    both_panel = both_panel + jnp.where(
        both_global[:, None] == panel_ids_all[None, :], shift_panel[None, :], 0.0
    )
    schur_tile = lax.dot_general(row_w, col_w, dims, preferred_element_type=f32)
    schur_tile = schur_tile + jnp.where(
        row_global[:, None] == col_global[None, :], shift_col[None, :], 0.0
    )

    inverse_factor_panel = inverse_cholesky(diag_block)
    solved = lax.dot_general(
        both_panel, inverse_factor_panel, dims, precision=high, preferred_element_type=f32
    )
    local_rows = row_global.shape[0]
    row_factor = solved[:local_rows]
    col_factor = solved[local_rows:]

    panel_piece = lax.dynamic_slice_in_dim(
        row_factor.reshape(local_rows, owners, slab), col_index * window, window, 2
    ).reshape(local_rows, owners * window)
    panel_cols_global = col_global.reshape(NPAN, -1)[0]
    finished = jnp.where(row_global[:, None] >= panel_cols_global[None, :], panel_piece, 0.0)

    boundary = PANELS * PW
    first_trailing = owners * window
    update = jnp.dot(
        row_factor, col_factor[first_trailing:].T, precision=high, preferred_element_type=f32
    )
    trailing = schur_tile[:, first_trailing:] - update
    trailing = jnp.where(row_global[:, None] >= boundary, trailing, 0.0)
    return jnp.concatenate([finished, trailing], axis=1)


def solution(mesh):
    in_specs = (
        P("grp", None, ("row", "col")),
        P("grp", None, None),
        P("grp"),
        P(("grp", "row", "col")),
    )
    out_specs = P(("grp", "row"), "col")
    return jax.shard_map(local, mesh=mesh, in_specs=in_specs, out_specs=out_specs, check_vma=False)
```

```python
import functools

import jax
import jax.numpy as jnp
from jax import lax
from jax.experimental import pallas as pl
from jax.experimental.pallas import tpu as pltpu
from jax.sharding import PartitionSpec as P

PW = 1024
PANELS = 1
NPAN = 10
HI = lax.Precision.HIGH
MESH = pl.DeviceIdType.MESH


def _gather_kernel(x_ref, out_ref, local_sem, send_sem, recv_sem, *, axis, count):
    me = lax.axis_index(axis)
    barrier = pltpu.get_barrier_semaphore()
    for step in range(1, count):
        peer = lax.rem(me + step, count)
        pl.semaphore_signal(barrier, inc=1, device_id={axis: peer}, device_id_type=MESH)
    pl.semaphore_wait(barrier, count - 1)
    own = pltpu.make_async_copy(x_ref, out_ref.at[me], local_sem)
    own.start()
    copies = []
    for step in range(1, count):
        peer = lax.rem(me + step, count)
        copy = pltpu.make_async_remote_copy(
            src_ref=x_ref,
            dst_ref=out_ref.at[me],
            send_sem=send_sem.at[step],
            recv_sem=recv_sem.at[step],
            device_id={axis: peer},
            device_id_type=MESH,
        )
        copy.start()
        copies.append(copy)
    own.wait()
    for copy in copies:
        copy.wait()


def remote_gather(x, axis, count, collective_id):
    return pl.pallas_call(
        functools.partial(_gather_kernel, axis=axis, count=count),
        out_shape=jax.ShapeDtypeStruct((count,) + x.shape, x.dtype),
        in_specs=[pl.BlockSpec(memory_space=pl.ANY)],
        out_specs=pl.BlockSpec(memory_space=pl.ANY),
        scratch_shapes=[
            pltpu.SemaphoreType.DMA(()),
            pltpu.SemaphoreType.DMA((count,)),
            pltpu.SemaphoreType.DMA((count,)),
        ],
        compiler_params=pltpu.CompilerParams(collective_id=collective_id, has_side_effects=True),
    )(x)


def _base_inverse(s):
    b = s.shape[0]
    lane = lax.broadcasted_iota(jnp.int32, (b, b), 1)
    sub = lax.broadcasted_iota(jnp.int32, (b, b), 0)
    sub_col = lax.broadcasted_iota(jnp.int32, (b, 1), 0)
    lane_row = lax.broadcasted_iota(jnp.int32, (1, b), 1)
    eye = jnp.where(lane == sub, 1.0, 0.0).astype(jnp.float32)

    width = 4

    def step(i, carry):
        work, inv = carry
        first = width * i
        rows = [jnp.sum(jnp.where(sub == first + q, work, 0.0), axis=0, keepdims=True)
                for q in range(width)]
        cols = [jnp.sum(jnp.where(lane == first + q, work, 0.0), axis=1, keepdims=True)
                for q in range(width)]
        invs = [jnp.sum(jnp.where(sub == first + q, inv, 0.0), axis=0, keepdims=True)
                for q in range(width)]
        block = [[jnp.sum(jnp.where(lane_row == first + r, rows[q], 0.0), axis=1, keepdims=True)
                  for r in range(width)] for q in range(width)]
        small = [[None] * width for _ in range(width)]
        scales = []
        for q in range(width):
            for p in range(q):
                acc = block[p][q]
                for t in range(p):
                    acc = acc - small[q][t] * small[p][t]
                small[q][p] = acc * scales[p]
            d = block[q][q]
            for t in range(q):
                d = d - small[q][t] * small[q][t]
            scales.append(lax.rsqrt(d))
        lcols, lrows, xrows = [], [], []
        for q in range(width):
            c, r, x = cols[q], rows[q], invs[q]
            for p in range(q):
                c = c - lcols[p] * small[q][p]
                r = r - lrows[p] * small[q][p]
                x = x - (small[q][p] * scales[p]) * xrows[p]
            lcols.append(jnp.where(sub_col >= first + q, c * scales[q], 0.0))
            lrows.append(jnp.where(lane_row >= first + q, r * scales[q], 0.0))
            xrows.append(x)
        for q in range(width):
            work = work - lcols[q] * lrows[q]
            u = jnp.where(sub_col == first + q, lcols[q] - 1.0, lcols[q]) * scales[q]
            inv = inv - u * xrows[q]
        return work, inv

    _, inv = lax.fori_loop(0, b // width, step, (s, eye))
    return inv


def _kernel(a_ref, z_ref, *, n, b):
    z_ref[...] = jnp.zeros_like(z_ref)
    for k in range(n // b):
        lo = k * b
        s = a_ref[lo:lo + b, lo:lo + b]
        if k > 0:
            zk = z_ref[0:lo, 0:lo]
            left = lax.dot_general(a_ref[lo:lo + b, 0:lo], zk, (((1,), (1,)), ((), ())),
                                   precision=HI, preferred_element_type=jnp.float32)
            s = s - lax.dot_general(left, left, (((1,), (1,)), ((), ())),
                                    precision=HI, preferred_element_type=jnp.float32)
        d = _base_inverse(s)
        z_ref[lo:lo + b, lo:lo + b] = d
        if k > 0:
            t = jnp.dot(left, zk, precision=HI, preferred_element_type=jnp.float32)
            z_ref[lo:lo + b, 0:lo] = -jnp.dot(d, t, precision=HI, preferred_element_type=jnp.float32)


def inverse_cholesky(a, b=128):
    n = a.shape[0]
    return pl.pallas_call(
        functools.partial(_kernel, n=n, b=b),
        out_shape=jax.ShapeDtypeStruct((n, n), jnp.float32),
        in_specs=[pl.BlockSpec(memory_space=pltpu.VMEM)],
        out_specs=pl.BlockSpec(memory_space=pltpu.VMEM),
        compiler_params=pltpu.CompilerParams(vmem_limit_bytes=48 * 1024 * 1024),
        cost_estimate=pl.CostEstimate(
            flops=2 * n * n * n, transcendentals=n, bytes_accessed=8 * n * n
        ),
    )(a)


def split3(x):
    hi = lax.reduce_precision(x, exponent_bits=8, mantissa_bits=7)
    rest = x - hi
    mid = lax.reduce_precision(rest, exponent_bits=8, mantissa_bits=7)
    lo = rest - mid
    return jnp.concatenate([hi, mid, lo]).astype(jnp.bfloat16)


def join3(parts):
    parts = parts.astype(jnp.float32).reshape(parts.shape[:-1] + (3, -1))
    return (parts[..., 0, :] + parts[..., 1, :]) + parts[..., 2, :]


def local(block_rows, inverse_factor, live_rows, shift):
    highest = lax.Precision.HIGHEST
    high = lax.Precision.HIGH
    groups = lax.axis_size("grp")
    rowcount = lax.axis_size("row")
    colcount = lax.axis_size("col")
    owners = groups * rowcount
    slab = PW // owners
    window = slab // colcount
    group_index = lax.axis_index("grp")
    row_index = lax.axis_index("row")
    col_index = lax.axis_index("col")
    blocks, padded, local_cols = block_rows.shape
    stacked = blocks * padded
    total = stacked * groups

    ordinal = jnp.arange(padded, dtype=jnp.int32)
    live_mask = (ordinal[None, :] < live_rows[:, None]).astype(jnp.float32)
    masked_factor = inverse_factor * live_mask[:, :, None] * live_mask[:, None, :]
    whitened = jnp.einsum(
        "bij,bjm->mbi", masked_factor, block_rows.astype(jnp.float32), precision=highest
    )
    whitened = whitened.astype(jnp.bfloat16).reshape(local_cols, stacked)

    shift_row = jnp.zeros((1, stacked), jnp.bfloat16).at[0, : 3 * shift.shape[0]].set(
        split3(shift)
    )
    every = lax.all_gather(
        jnp.concatenate([whitened, shift_row], axis=0), "grp", axis=0, tiled=False
    )
    shift_grp = join3(every[:, local_cols, : 3 * shift.shape[0]]).reshape(groups, NPAN, window)
    every = jnp.transpose(every[:, :local_cols], (1, 0, 2)).reshape(groups, NPAN, window, total)

    panel_shift_row = jnp.zeros((1, total), jnp.bfloat16).at[0, : 3 * groups * window].set(
        split3(shift_grp[:, 0].reshape(-1))
    )
    panel_w = jnp.concatenate([every[:, 0].reshape(groups * window, total), panel_shift_row], 0)
    col_w = lax.all_gather(every, "row", axis=0, tiled=False)
    panel_w = remote_gather(panel_w, "col", colcount, 0)
    panel_w, col_w = lax.optimization_barrier((panel_w, col_w))
    panel_w = lax.all_gather(panel_w, "row", axis=0, tiled=False)
    col_w = jnp.transpose(col_w, (2, 1, 0, 3, 4)).reshape(NPAN * owners * window, total)
    every, panel_w, col_w = lax.optimization_barrier((every, panel_w, col_w))
    shift_panel = join3(panel_w[:, :, groups * window, : 3 * groups * window])
    shift_panel = jnp.transpose(
        shift_panel.reshape(rowcount, colcount, groups, window), (2, 0, 1, 3)
    ).reshape(PW)
    panel_w = panel_w[:, :, : groups * window].reshape(rowcount, colcount, groups, window, total)
    panel_w = jnp.transpose(panel_w, (2, 0, 1, 3, 4)).reshape(PW, total)

    row_w = lax.dynamic_index_in_dim(every, group_index, 0, keepdims=False)
    row_w = lax.all_gather(row_w, "col", axis=0, tiled=False)
    row_w = jnp.transpose(row_w, (1, 0, 2, 3)).reshape(NPAN * colcount * window, total)

    panel_ids = jnp.arange(NPAN, dtype=jnp.int32)
    slab_ids = jnp.arange(slab, dtype=jnp.int32)
    owner_ids = jnp.arange(owners, dtype=jnp.int32)
    window_ids = jnp.arange(window, dtype=jnp.int32)
    own_owner = group_index * rowcount + row_index
    row_global = ((panel_ids[:, None] * owners + own_owner) * slab + slab_ids[None, :]).reshape(-1)
    col_global = (
        (panel_ids[:, None, None] * owners + owner_ids[None, :, None]) * slab
        + col_index * window
        + window_ids[None, None, :]
    ).reshape(-1)
    panel_ids_all = jnp.arange(PW, dtype=jnp.int32)
    shift_col = jnp.broadcast_to(
        shift.reshape(NPAN, 1, window), (NPAN, owners, window)
    ).reshape(-1)

    dims = (((1,), (1,)), ((), ()))
    f32 = jnp.float32
    diag_block = lax.dot_general(panel_w, panel_w, dims, preferred_element_type=f32)
    diag_block = diag_block + jnp.where(
        panel_ids_all[:, None] == panel_ids_all[None, :], shift_panel[None, :], 0.0
    )
    both_w = jnp.concatenate([row_w, col_w], axis=0)
    both_global = jnp.concatenate([row_global, col_global], axis=0)
    both_panel = lax.dot_general(both_w, panel_w, dims, preferred_element_type=f32)
    both_panel = both_panel + jnp.where(
        both_global[:, None] == panel_ids_all[None, :], shift_panel[None, :], 0.0
    )
    schur_tile = lax.dot_general(row_w, col_w, dims, preferred_element_type=f32)
    schur_tile = schur_tile + jnp.where(
        row_global[:, None] == col_global[None, :], shift_col[None, :], 0.0
    )

    inverse_factor_panel = inverse_cholesky(diag_block)
    solved = lax.dot_general(
        both_panel, inverse_factor_panel, dims, precision=high, preferred_element_type=f32
    )
    local_rows = row_global.shape[0]
    row_factor = solved[:local_rows]
    col_factor = solved[local_rows:]

    panel_piece = lax.dynamic_slice_in_dim(
        row_factor.reshape(local_rows, owners, slab), col_index * window, window, 2
    ).reshape(local_rows, owners * window)
    panel_cols_global = col_global.reshape(NPAN, -1)[0]
    finished = jnp.where(row_global[:, None] >= panel_cols_global[None, :], panel_piece, 0.0)

    boundary = PANELS * PW
    first_trailing = owners * window
    update = jnp.dot(
        row_factor, col_factor[first_trailing:].T, precision=high, preferred_element_type=f32
    )
    trailing = schur_tile[:, first_trailing:] - update
    trailing = jnp.where(row_global[:, None] >= boundary, trailing, 0.0)
    return jnp.concatenate([finished, trailing], axis=1)


def solution(mesh):
    in_specs = (
        P("grp", None, ("row", "col")),
        P("grp", None, None),
        P("grp"),
        P(("grp", "row", "col")),
    )
    out_specs = P(("grp", "row"), "col")
    return jax.shard_map(local, mesh=mesh, in_specs=in_specs, out_specs=out_specs, check_vma=False)
```

```python
import functools

import jax
import jax.numpy as jnp
from jax import lax
from jax.experimental import pallas as pl
from jax.experimental.pallas import tpu as pltpu
from jax.sharding import PartitionSpec as P

PW = 1024
PANELS = 1
NPAN = 10
HI = lax.Precision.HIGH
MESH = pl.DeviceIdType.MESH


def _gather_kernel(x_ref, out_ref, local_sem, send_sem, recv_sem, *, axis, count):
    me = lax.axis_index(axis)
    barrier = pltpu.get_barrier_semaphore()
    for step in range(1, count):
        peer = lax.rem(me + step, count)
        pl.semaphore_signal(barrier, inc=1, device_id={axis: peer}, device_id_type=MESH)
    pl.semaphore_wait(barrier, count - 1)
    own = pltpu.make_async_copy(x_ref, out_ref.at[me], local_sem)
    own.start()
    copies = []
    for step in range(1, count):
        peer = lax.rem(me + step, count)
        copy = pltpu.make_async_remote_copy(
            src_ref=x_ref,
            dst_ref=out_ref.at[me],
            send_sem=send_sem.at[step],
            recv_sem=recv_sem.at[step],
            device_id={axis: peer},
            device_id_type=MESH,
        )
        copy.start()
        copies.append(copy)
    own.wait()
    for copy in copies:
        copy.wait()


def remote_gather(x, axis, count, collective_id):
    return pl.pallas_call(
        functools.partial(_gather_kernel, axis=axis, count=count),
        out_shape=jax.ShapeDtypeStruct((count,) + x.shape, x.dtype),
        in_specs=[pl.BlockSpec(memory_space=pl.ANY)],
        out_specs=pl.BlockSpec(memory_space=pl.ANY),
        scratch_shapes=[
            pltpu.SemaphoreType.DMA(()),
            pltpu.SemaphoreType.DMA((count,)),
            pltpu.SemaphoreType.DMA((count,)),
        ],
        compiler_params=pltpu.CompilerParams(collective_id=collective_id, has_side_effects=True),
    )(x)


def _base_inverse(s):
    b = s.shape[0]
    lane = lax.broadcasted_iota(jnp.int32, (b, b), 1)
    sub = lax.broadcasted_iota(jnp.int32, (b, b), 0)
    sub_col = lax.broadcasted_iota(jnp.int32, (b, 1), 0)
    lane_row = lax.broadcasted_iota(jnp.int32, (1, b), 1)
    eye = jnp.where(lane == sub, 1.0, 0.0).astype(jnp.float32)

    width = 4

    def step(i, carry):
        work, inv = carry
        first = width * i
        rows = [jnp.sum(jnp.where(sub == first + q, work, 0.0), axis=0, keepdims=True)
                for q in range(width)]
        cols = [jnp.sum(jnp.where(lane == first + q, work, 0.0), axis=1, keepdims=True)
                for q in range(width)]
        invs = [jnp.sum(jnp.where(sub == first + q, inv, 0.0), axis=0, keepdims=True)
                for q in range(width)]
        block = [[jnp.sum(jnp.where(lane_row == first + r, rows[q], 0.0), axis=1, keepdims=True)
                  for r in range(width)] for q in range(width)]
        small = [[None] * width for _ in range(width)]
        scales = []
        for q in range(width):
            for p in range(q):
                acc = block[p][q]
                for t in range(p):
                    acc = acc - small[q][t] * small[p][t]
                small[q][p] = acc * scales[p]
            d = block[q][q]
            for t in range(q):
                d = d - small[q][t] * small[q][t]
            scales.append(lax.rsqrt(d))
        lcols, lrows, xrows = [], [], []
        for q in range(width):
            c, r, x = cols[q], rows[q], invs[q]
            for p in range(q):
                c = c - lcols[p] * small[q][p]
                r = r - lrows[p] * small[q][p]
                x = x - (small[q][p] * scales[p]) * xrows[p]
            lcols.append(jnp.where(sub_col >= first + q, c * scales[q], 0.0))
            lrows.append(jnp.where(lane_row >= first + q, r * scales[q], 0.0))
            xrows.append(x)
        for q in range(width):
            work = work - lcols[q] * lrows[q]
            u = jnp.where(sub_col == first + q, lcols[q] - 1.0, lcols[q]) * scales[q]
            inv = inv - u * xrows[q]
        return work, inv

    _, inv = lax.fori_loop(0, b // width, step, (s, eye))
    return inv


def _kernel(a_ref, z_ref, *, n, b):
    z_ref[...] = jnp.zeros_like(z_ref)
    for k in range(n // b):
        lo = k * b
        s = a_ref[lo:lo + b, lo:lo + b]
        if k > 0:
            zk = z_ref[0:lo, 0:lo]
            left = lax.dot_general(a_ref[lo:lo + b, 0:lo], zk, (((1,), (1,)), ((), ())),
                                   precision=HI, preferred_element_type=jnp.float32)
            s = s - lax.dot_general(left, left, (((1,), (1,)), ((), ())),
                                    precision=HI, preferred_element_type=jnp.float32)
        d = _base_inverse(s)
        z_ref[lo:lo + b, lo:lo + b] = d
        if k > 0:
            t = jnp.dot(left, zk, precision=HI, preferred_element_type=jnp.float32)
            z_ref[lo:lo + b, 0:lo] = -jnp.dot(d, t, precision=HI, preferred_element_type=jnp.float32)


def inverse_cholesky(a, b=128):
    n = a.shape[0]
    return pl.pallas_call(
        functools.partial(_kernel, n=n, b=b),
        out_shape=jax.ShapeDtypeStruct((n, n), jnp.float32),
        in_specs=[pl.BlockSpec(memory_space=pltpu.VMEM)],
        out_specs=pl.BlockSpec(memory_space=pltpu.VMEM),
        compiler_params=pltpu.CompilerParams(vmem_limit_bytes=48 * 1024 * 1024),
        cost_estimate=pl.CostEstimate(
            flops=2 * n * n * n, transcendentals=n, bytes_accessed=8 * n * n
        ),
    )(a)


def split3(x):
    hi = lax.reduce_precision(x, exponent_bits=8, mantissa_bits=7)
    rest = x - hi
    mid = lax.reduce_precision(rest, exponent_bits=8, mantissa_bits=7)
    lo = rest - mid
    return jnp.concatenate([hi, mid, lo]).astype(jnp.bfloat16)


def join3(parts):
    parts = parts.astype(jnp.float32).reshape(parts.shape[:-1] + (3, -1))
    return (parts[..., 0, :] + parts[..., 1, :]) + parts[..., 2, :]


def local(block_rows, inverse_factor, live_rows, shift):
    highest = lax.Precision.HIGHEST
    high = lax.Precision.HIGH
    groups = lax.axis_size("grp")
    rowcount = lax.axis_size("row")
    colcount = lax.axis_size("col")
    owners = groups * rowcount
    slab = PW // owners
    window = slab // colcount
    group_index = lax.axis_index("grp")
    row_index = lax.axis_index("row")
    col_index = lax.axis_index("col")
    blocks, padded, local_cols = block_rows.shape
    stacked = blocks * padded
    total = stacked * groups

    ordinal = jnp.arange(padded, dtype=jnp.int32)
    live_mask = (ordinal[None, :] < live_rows[:, None]).astype(jnp.float32)
    masked_factor = inverse_factor * live_mask[:, :, None] * live_mask[:, None, :]
    whitened = jnp.einsum(
        "bij,bjm->mbi", masked_factor, block_rows.astype(jnp.float32), precision=highest
    )
    whitened = whitened.astype(jnp.bfloat16).reshape(local_cols, stacked)

    shift_row = jnp.zeros((1, stacked), jnp.bfloat16).at[0, : 3 * shift.shape[0]].set(
        split3(shift)
    )
    every = lax.all_gather(
        jnp.concatenate([whitened, shift_row], axis=0), "grp", axis=0, tiled=False
    )
    shift_grp = join3(every[:, local_cols, : 3 * shift.shape[0]]).reshape(groups, NPAN, window)
    every = jnp.transpose(every[:, :local_cols], (1, 0, 2)).reshape(groups, NPAN, window, total)

    panel_shift_row = jnp.zeros((1, total), jnp.bfloat16).at[0, : 3 * groups * window].set(
        split3(shift_grp[:, 0].reshape(-1))
    )
    panel_w = jnp.concatenate([every[:, 0].reshape(groups * window, total), panel_shift_row], 0)
    col_w = lax.all_gather(every, "row", axis=0, tiled=False)
    panel_w = remote_gather(panel_w, "col", colcount, 0)
    panel_w, col_w = lax.optimization_barrier((panel_w, col_w))
    split = 10 * 128
    first_half = lax.all_gather(panel_w[:, :, :split], "row", axis=0, tiled=False)
    second_half = lax.all_gather(panel_w[:, :, split:], "row", axis=0, tiled=False)
    col_w = jnp.transpose(col_w, (2, 1, 0, 3, 4)).reshape(NPAN * owners * window, total)
    shift_panel = join3(first_half[:, :, groups * window, : 3 * groups * window])
    shift_panel = jnp.transpose(
        shift_panel.reshape(rowcount, colcount, groups, window), (2, 0, 1, 3)
    ).reshape(PW)

    def natural(half):
        half = half[:, :, : groups * window].reshape(
            rowcount, colcount, groups, window, half.shape[-1]
        )
        return jnp.transpose(half, (2, 0, 1, 3, 4)).reshape(PW, half.shape[-1])

    first_half = natural(first_half)
    dims_half = (((1,), (1,)), ((), ()))
    first_block = lax.dot_general(first_half, first_half, dims_half, preferred_element_type=jnp.float32)
    every, second_half, col_w = lax.optimization_barrier((every, second_half, col_w))
    second_half = natural(second_half)
    panel_w = jnp.concatenate([first_half, second_half], axis=1)

    row_w = lax.dynamic_index_in_dim(every, group_index, 0, keepdims=False)
    row_w = lax.all_gather(row_w, "col", axis=0, tiled=False)
    row_w = jnp.transpose(row_w, (1, 0, 2, 3)).reshape(NPAN * colcount * window, total)

    panel_ids = jnp.arange(NPAN, dtype=jnp.int32)
    slab_ids = jnp.arange(slab, dtype=jnp.int32)
    owner_ids = jnp.arange(owners, dtype=jnp.int32)
    window_ids = jnp.arange(window, dtype=jnp.int32)
    own_owner = group_index * rowcount + row_index
    row_global = ((panel_ids[:, None] * owners + own_owner) * slab + slab_ids[None, :]).reshape(-1)
    col_global = (
        (panel_ids[:, None, None] * owners + owner_ids[None, :, None]) * slab
        + col_index * window
        + window_ids[None, None, :]
    ).reshape(-1)
    panel_ids_all = jnp.arange(PW, dtype=jnp.int32)
    shift_col = jnp.broadcast_to(
        shift.reshape(NPAN, 1, window), (NPAN, owners, window)
    ).reshape(-1)

    dims = (((1,), (1,)), ((), ()))
    f32 = jnp.float32
    diag_block = first_block + lax.dot_general(
        second_half, second_half, dims, preferred_element_type=f32
    )
    diag_block = diag_block + jnp.where(
        panel_ids_all[:, None] == panel_ids_all[None, :], shift_panel[None, :], 0.0
    )
    both_w = jnp.concatenate([row_w, col_w], axis=0)
    both_global = jnp.concatenate([row_global, col_global], axis=0)
    both_panel = lax.dot_general(both_w, panel_w, dims, preferred_element_type=f32)
    both_panel = both_panel + jnp.where(
        both_global[:, None] == panel_ids_all[None, :], shift_panel[None, :], 0.0
    )
    schur_tile = lax.dot_general(row_w, col_w, dims, preferred_element_type=f32)
    schur_tile = schur_tile + jnp.where(
        row_global[:, None] == col_global[None, :], shift_col[None, :], 0.0
    )

    inverse_factor_panel = inverse_cholesky(diag_block)
    solved = lax.dot_general(
        both_panel, inverse_factor_panel, dims, precision=high, preferred_element_type=f32
    )
    local_rows = row_global.shape[0]
    row_factor = solved[:local_rows]
    col_factor = solved[local_rows:]

    panel_piece = lax.dynamic_slice_in_dim(
        row_factor.reshape(local_rows, owners, slab), col_index * window, window, 2
    ).reshape(local_rows, owners * window)
    panel_cols_global = col_global.reshape(NPAN, -1)[0]
    finished = jnp.where(row_global[:, None] >= panel_cols_global[None, :], panel_piece, 0.0)

    boundary = PANELS * PW
    first_trailing = owners * window
    update = jnp.dot(
        row_factor, col_factor[first_trailing:].T, precision=high, preferred_element_type=f32
    )
    trailing = schur_tile[:, first_trailing:] - update
    trailing = jnp.where(row_global[:, None] >= boundary, trailing, 0.0)
    return jnp.concatenate([finished, trailing], axis=1)


def solution(mesh):
    in_specs = (
        P("grp", None, ("row", "col")),
        P("grp", None, None),
        P("grp"),
        P(("grp", "row", "col")),
    )
    out_specs = P(("grp", "row"), "col")
    return jax.shard_map(local, mesh=mesh, in_specs=in_specs, out_specs=out_specs, check_vma=False)
```

```python
import functools

import jax
import jax.numpy as jnp
from jax import lax
from jax.experimental import pallas as pl
from jax.experimental.pallas import tpu as pltpu
from jax.sharding import PartitionSpec as P

PW = 1024
PANELS = 1
NPAN = 10
HI = lax.Precision.HIGH
MESH = pl.DeviceIdType.MESH


def _gather_kernel(x_ref, out_ref, local_sem, send_sem, recv_sem, *, axis, count):
    me = lax.axis_index(axis)
    barrier = pltpu.get_barrier_semaphore()
    for step in range(1, count):
        peer = lax.rem(me + step, count)
        pl.semaphore_signal(barrier, inc=1, device_id={axis: peer}, device_id_type=MESH)
    pl.semaphore_wait(barrier, count - 1)
    own = pltpu.make_async_copy(x_ref, out_ref.at[me], local_sem)
    own.start()
    copies = []
    for step in range(1, count):
        peer = lax.rem(me + step, count)
        copy = pltpu.make_async_remote_copy(
            src_ref=x_ref,
            dst_ref=out_ref.at[me],
            send_sem=send_sem.at[step],
            recv_sem=recv_sem.at[step],
            device_id={axis: peer},
            device_id_type=MESH,
        )
        copy.start()
        copies.append(copy)
    own.wait()
    for copy in copies:
        copy.wait()


def remote_gather(x, axis, count, collective_id):
    return pl.pallas_call(
        functools.partial(_gather_kernel, axis=axis, count=count),
        out_shape=jax.ShapeDtypeStruct((count,) + x.shape, x.dtype),
        in_specs=[pl.BlockSpec(memory_space=pl.ANY)],
        out_specs=pl.BlockSpec(memory_space=pl.ANY),
        scratch_shapes=[
            pltpu.SemaphoreType.DMA(()),
            pltpu.SemaphoreType.DMA((count,)),
            pltpu.SemaphoreType.DMA((count,)),
        ],
        compiler_params=pltpu.CompilerParams(collective_id=collective_id, has_side_effects=True),
    )(x)


def _base_inverse(s):
    b = s.shape[0]
    lane = lax.broadcasted_iota(jnp.int32, (b, b), 1)
    sub = lax.broadcasted_iota(jnp.int32, (b, b), 0)
    sub_col = lax.broadcasted_iota(jnp.int32, (b, 1), 0)
    lane_row = lax.broadcasted_iota(jnp.int32, (1, b), 1)
    eye = jnp.where(lane == sub, 1.0, 0.0).astype(jnp.float32)

    width = 4

    def step(i, carry):
        work, inv = carry
        first = width * i
        rows = [jnp.sum(jnp.where(sub == first + q, work, 0.0), axis=0, keepdims=True)
                for q in range(width)]
        cols = [jnp.sum(jnp.where(lane == first + q, work, 0.0), axis=1, keepdims=True)
                for q in range(width)]
        invs = [jnp.sum(jnp.where(sub == first + q, inv, 0.0), axis=0, keepdims=True)
                for q in range(width)]
        block = [[jnp.sum(jnp.where(lane_row == first + r, rows[q], 0.0), axis=1, keepdims=True)
                  for r in range(width)] for q in range(width)]
        small = [[None] * width for _ in range(width)]
        scales = []
        for q in range(width):
            for p in range(q):
                acc = block[p][q]
                for t in range(p):
                    acc = acc - small[q][t] * small[p][t]
                small[q][p] = acc * scales[p]
            d = block[q][q]
            for t in range(q):
                d = d - small[q][t] * small[q][t]
            scales.append(lax.rsqrt(d))
        lcols, lrows, xrows = [], [], []
        for q in range(width):
            c, r, x = cols[q], rows[q], invs[q]
            for p in range(q):
                c = c - lcols[p] * small[q][p]
                r = r - lrows[p] * small[q][p]
                x = x - (small[q][p] * scales[p]) * xrows[p]
            lcols.append(jnp.where(sub_col >= first + q, c * scales[q], 0.0))
            lrows.append(jnp.where(lane_row >= first + q, r * scales[q], 0.0))
            xrows.append(x)
        for q in range(width):
            work = work - lcols[q] * lrows[q]
            u = jnp.where(sub_col == first + q, lcols[q] - 1.0, lcols[q]) * scales[q]
            inv = inv - u * xrows[q]
        return work, inv

    _, inv = lax.fori_loop(0, b // width, step, (s, eye))
    return inv


def _kernel(a_ref, z_ref, *, n, b):
    z_ref[...] = jnp.zeros_like(z_ref)
    for k in range(n // b):
        lo = k * b
        s = a_ref[lo:lo + b, lo:lo + b]
        if k > 0:
            zk = z_ref[0:lo, 0:lo]
            left = lax.dot_general(a_ref[lo:lo + b, 0:lo], zk, (((1,), (1,)), ((), ())),
                                   precision=HI, preferred_element_type=jnp.float32)
            s = s - lax.dot_general(left, left, (((1,), (1,)), ((), ())),
                                    precision=HI, preferred_element_type=jnp.float32)
        d = _base_inverse(s)
        z_ref[lo:lo + b, lo:lo + b] = d
        if k > 0:
            t = jnp.dot(left, zk, precision=HI, preferred_element_type=jnp.float32)
            z_ref[lo:lo + b, 0:lo] = -jnp.dot(d, t, precision=HI, preferred_element_type=jnp.float32)


def inverse_cholesky(a, b=128):
    n = a.shape[0]
    return pl.pallas_call(
        functools.partial(_kernel, n=n, b=b),
        out_shape=jax.ShapeDtypeStruct((n, n), jnp.float32),
        in_specs=[pl.BlockSpec(memory_space=pltpu.VMEM)],
        out_specs=pl.BlockSpec(memory_space=pltpu.VMEM),
        compiler_params=pltpu.CompilerParams(vmem_limit_bytes=48 * 1024 * 1024),
        cost_estimate=pl.CostEstimate(
            flops=2 * n * n * n, transcendentals=n, bytes_accessed=8 * n * n
        ),
    )(a)


def split3(x):
    hi = lax.reduce_precision(x, exponent_bits=8, mantissa_bits=7)
    rest = x - hi
    mid = lax.reduce_precision(rest, exponent_bits=8, mantissa_bits=7)
    lo = rest - mid
    return jnp.concatenate([hi, mid, lo]).astype(jnp.bfloat16)


def join3(parts):
    parts = parts.astype(jnp.float32).reshape(parts.shape[:-1] + (3, -1))
    return (parts[..., 0, :] + parts[..., 1, :]) + parts[..., 2, :]


def local(block_rows, inverse_factor, live_rows, shift):
    highest = lax.Precision.HIGHEST
    high = lax.Precision.HIGH
    groups = lax.axis_size("grp")
    rowcount = lax.axis_size("row")
    colcount = lax.axis_size("col")
    owners = groups * rowcount
    slab = PW // owners
    window = slab // colcount
    group_index = lax.axis_index("grp")
    row_index = lax.axis_index("row")
    col_index = lax.axis_index("col")
    blocks, padded, local_cols = block_rows.shape
    stacked = blocks * padded
    total = stacked * groups

    ordinal = jnp.arange(padded, dtype=jnp.int32)
    live_mask = (ordinal[None, :] < live_rows[:, None]).astype(jnp.float32)
    masked_factor = inverse_factor * live_mask[:, :, None] * live_mask[:, None, :]
    whitened = jnp.einsum(
        "bij,bjm->mbi", masked_factor, block_rows.astype(jnp.float32), precision=highest
    )
    whitened = whitened.astype(jnp.bfloat16).reshape(local_cols, stacked)

    shift_row = jnp.zeros((1, stacked), jnp.bfloat16).at[0, : 3 * shift.shape[0]].set(
        split3(shift)
    )
    every = remote_gather(jnp.concatenate([whitened, shift_row], axis=0), "grp", groups, 2)
    shift_grp = join3(every[:, local_cols, : 3 * shift.shape[0]]).reshape(groups, NPAN, window)
    every = jnp.transpose(every[:, :local_cols], (1, 0, 2)).reshape(groups, NPAN, window, total)

    panel_shift_row = jnp.zeros((1, total), jnp.bfloat16).at[0, : 3 * groups * window].set(
        split3(shift_grp[:, 0].reshape(-1))
    )
    panel_w = jnp.concatenate([every[:, 0].reshape(groups * window, total), panel_shift_row], 0)
    col_w = lax.all_gather(every, "row", axis=0, tiled=False)
    panel_w = remote_gather(panel_w, "col", colcount, 0)
    panel_w, col_w = lax.optimization_barrier((panel_w, col_w))
    split = 10 * 128
    first_half = lax.all_gather(panel_w[:, :, :split], "row", axis=0, tiled=False)
    second_half = lax.all_gather(panel_w[:, :, split:], "row", axis=0, tiled=False)
    col_w = jnp.transpose(col_w, (2, 1, 0, 3, 4)).reshape(NPAN * owners * window, total)
    shift_panel = join3(first_half[:, :, groups * window, : 3 * groups * window])
    shift_panel = jnp.transpose(
        shift_panel.reshape(rowcount, colcount, groups, window), (2, 0, 1, 3)
    ).reshape(PW)

    def natural(half):
        half = half[:, :, : groups * window].reshape(
            rowcount, colcount, groups, window, half.shape[-1]
        )
        return jnp.transpose(half, (2, 0, 1, 3, 4)).reshape(PW, half.shape[-1])

    first_half = natural(first_half)
    dims_half = (((1,), (1,)), ((), ()))
    first_block = lax.dot_general(first_half, first_half, dims_half, preferred_element_type=jnp.float32)
    every, second_half, col_w = lax.optimization_barrier((every, second_half, col_w))
    second_half = natural(second_half)
    panel_w = jnp.concatenate([first_half, second_half], axis=1)

    row_w = lax.dynamic_index_in_dim(every, group_index, 0, keepdims=False)
    row_w = lax.all_gather(row_w, "col", axis=0, tiled=False)
    row_w = jnp.transpose(row_w, (1, 0, 2, 3)).reshape(NPAN * colcount * window, total)

    panel_ids = jnp.arange(NPAN, dtype=jnp.int32)
    slab_ids = jnp.arange(slab, dtype=jnp.int32)
    owner_ids = jnp.arange(owners, dtype=jnp.int32)
    window_ids = jnp.arange(window, dtype=jnp.int32)
    own_owner = group_index * rowcount + row_index
    row_global = ((panel_ids[:, None] * owners + own_owner) * slab + slab_ids[None, :]).reshape(-1)
    col_global = (
        (panel_ids[:, None, None] * owners + owner_ids[None, :, None]) * slab
        + col_index * window
        + window_ids[None, None, :]
    ).reshape(-1)
    panel_ids_all = jnp.arange(PW, dtype=jnp.int32)
    shift_col = jnp.broadcast_to(
        shift.reshape(NPAN, 1, window), (NPAN, owners, window)
    ).reshape(-1)

    dims = (((1,), (1,)), ((), ()))
    f32 = jnp.float32
    diag_block = first_block + lax.dot_general(
        second_half, second_half, dims, preferred_element_type=f32
    )
    diag_block = diag_block + jnp.where(
        panel_ids_all[:, None] == panel_ids_all[None, :], shift_panel[None, :], 0.0
    )
    both_w = jnp.concatenate([row_w, col_w], axis=0)
    both_global = jnp.concatenate([row_global, col_global], axis=0)
    both_panel = lax.dot_general(both_w, panel_w, dims, preferred_element_type=f32)
    both_panel = both_panel + jnp.where(
        both_global[:, None] == panel_ids_all[None, :], shift_panel[None, :], 0.0
    )
    schur_tile = lax.dot_general(row_w, col_w, dims, preferred_element_type=f32)
    schur_tile = schur_tile + jnp.where(
        row_global[:, None] == col_global[None, :], shift_col[None, :], 0.0
    )

    inverse_factor_panel = inverse_cholesky(diag_block)
    solved = lax.dot_general(
        both_panel, inverse_factor_panel, dims, precision=high, preferred_element_type=f32
    )
    local_rows = row_global.shape[0]
    row_factor = solved[:local_rows]
    col_factor = solved[local_rows:]

    panel_piece = lax.dynamic_slice_in_dim(
        row_factor.reshape(local_rows, owners, slab), col_index * window, window, 2
    ).reshape(local_rows, owners * window)
    panel_cols_global = col_global.reshape(NPAN, -1)[0]
    finished = jnp.where(row_global[:, None] >= panel_cols_global[None, :], panel_piece, 0.0)

    boundary = PANELS * PW
    first_trailing = owners * window
    update = jnp.dot(
        row_factor, col_factor[first_trailing:].T, precision=high, preferred_element_type=f32
    )
    trailing = schur_tile[:, first_trailing:] - update
    trailing = jnp.where(row_global[:, None] >= boundary, trailing, 0.0)
    return jnp.concatenate([finished, trailing], axis=1)


def solution(mesh):
    in_specs = (
        P("grp", None, ("row", "col")),
        P("grp", None, None),
        P("grp"),
        P(("grp", "row", "col")),
    )
    out_specs = P(("grp", "row"), "col")
    return jax.shard_map(local, mesh=mesh, in_specs=in_specs, out_specs=out_specs, check_vma=False)
```
